32 devices in a mesh: groups: 2 (over x), seq: 16 (over z, y, core).
Axes of the slice: x: 2, y: 2, z: 4, core: 2. Of those that a mesh axis runs over, the one named last changes fastest.
Arguments:
- queries: bfloat16 [4096, 2048], P(('groups', 'seq')), parts along dimension 0, may hold values from -8 to 8
- key_input: bfloat16 [4096, 2048], P(('groups', 'seq')), parts along dimension 0, may hold values from -4.5 to 4.5
- value_input: bfloat16 [4096, 2048], P(('groups', 'seq')), parts along dimension 0, may hold values from -6 to 6
- cotangent: bfloat16 [4096, 2048], P(('groups', 'seq')), parts along dimension 0, may hold values from -6 to 6
Outputs:
- attended: bfloat16 [4096, 2048], P(('groups', 'seq')), parts along dimension 0
- grad_queries: bfloat16 [4096, 2048], P(('groups', 'seq')), parts along dimension 0
- grad_keys: bfloat16 [4096, 2048], P(('groups', 'seq')), parts along dimension 0
- grad_values: bfloat16 [4096, 2048], P(('groups', 'seq')), parts along dimension 0
The draws below stay inside these ranges and needn't reach their ends.
There are 2 independent parts, one for each index of `groups`. The reference program is written for one: setup_inputs(seed, part) draws one part's arguments, and reference() takes and returns one part's arrays. A program takes and returns all parts, laid end to end along the dimension named above; each array names one. Nothing has to cross between parts.
All inputs are finite; a program needn't handle non-finite values.
Results may differ from the reference program's by a relative error of at most 0.024.
Values may be sent and summed in bfloat16 or wider, within the bound.
A program may use at most 128 MiB of HBM per device.

```python
import functools
import math
import jax
import jax.numpy as jnp
from jax import lax

HEADS = 16
HEAD_DIM = 128
BLOCK = 64
LEVELS = 3
SEQ_LEN = 2048


def paired_draw(key):
    feat_width = HEADS * HEAD_DIM
    query_key = jax.random.fold_in(key, 11)
    keys_key = jax.random.fold_in(key, 12)
    query_draw = jnp.clip(2.0 * jax.random.normal(query_key, (SEQ_LEN, feat_width), jnp.float32), -8.0, 8.0)
    keys_draw = jnp.clip(jax.random.normal(keys_key, (SEQ_LEN, feat_width), jnp.float32), -4.5, 4.5)
    return (query_draw, keys_draw)


def draw_queries(key, part):
    return paired_draw(key)[0].astype(jnp.bfloat16)


def draw_key_input(key, part):
    return paired_draw(key)[1].astype(jnp.bfloat16)


def block_scale(own_key, extent, cuts, least, high):
    level = 1.0
    for dim, shards_of in cuts:
        heights = jax.random.uniform(jax.random.fold_in(jax.random.fold_in(own_key, 6), dim), (shards_of,), jnp.float32, least / len(cuts), high / len(cuts))
        level = level * jnp.repeat(jnp.exp(heights), extent[dim] // shards_of).reshape((-1,) + (1,) * (len(extent) - 1 - dim))
    return level


def normal_values(own_key, extent, scale, limit, cuts=(), held_as=jnp.bfloat16):
    array = jax.random.normal(own_key, extent, jnp.float32) * scale
    if len(cuts) > 0:
        array = block_scale(own_key, extent, cuts, -0.22, 0.18) * array
    return jnp.clip(array, min=-limit, max=limit).astype(held_as)


def setup_inputs(seed: int = 0, part: int = 0) -> dict:
    key_of = jax.random.split(jax.random.key(seed), 5)
    part_keys = jax.random.split(jax.random.fold_in(key_of[4], part), 5)
    queries = draw_queries(jax.random.fold_in(jax.random.fold_in(key_of[4], part), 71), part)
    key_input = draw_key_input(jax.random.fold_in(jax.random.fold_in(key_of[4], part), 71), part)
    value_input = normal_values(part_keys[2], (SEQ_LEN, HEADS * HEAD_DIM), 1.0, 6.0, ((0, 16),))
    cotangent = normal_values(part_keys[3], (SEQ_LEN, HEADS * HEAD_DIM), 1.0, 6.0, ((0, 16),))
    return dict(queries=queries, key_input=key_input, value_input=value_input, cotangent=cotangent)


log_two = math.log(2.0)
masked_score = -1.0e30


def halve_rows(rows_in):
    wide = rows_in.astype(jnp.float32).reshape(rows_in.shape[0] // 2, 2, rows_in.shape[1])
    return ((wide[:, 0] + wide[:, 1]) * 0.5).astype(jnp.bfloat16)


def reference(queries, key_input, value_input, cotangent):
    feat_width = HEADS * HEAD_DIM
    scale = HEAD_DIM ** -0.5
    block_total = SEQ_LEN // BLOCK
    key_levels = [key_input]
    value_levels = [value_input]
    for height in range(1, LEVELS):
        key_levels.append(halve_rows(key_levels[-1]))
        value_levels.append(halve_rows(value_levels[-1]))
    key_padded = [jnp.pad(x, ((BLOCK, BLOCK), (0, 0))) for x in key_levels]
    value_padded = [jnp.pad(x, ((BLOCK, BLOCK), (0, 0))) for x in value_levels]
    acc_keys = [jnp.zeros(x.shape, jnp.float32) for x in key_padded]
    acc_values = [jnp.zeros(x.shape, jnp.float32) for x in value_padded]
    col_block = jnp.arange(3 * BLOCK) // BLOCK

    def advance(carry, block_no):
        acc_k, acc_v = carry
        start = (block_no * BLOCK).astype(jnp.int32)
        query_heads = lax.dynamic_slice_in_dim(queries, start, BLOCK, 0).astype(jnp.float32).reshape(BLOCK, HEADS, HEAD_DIM)
        grad_heads = lax.dynamic_slice_in_dim(cotangent, start, BLOCK, 0).astype(jnp.float32).reshape(BLOCK, HEADS, HEAD_DIM)
        score_list = []
        key_list = []
        value_list = []
        starts = []
        for height in range(LEVELS):
            coarse_no = jnp.right_shift(block_no, height)
            first_row = (coarse_no * BLOCK).astype(jnp.int32)
            key_rows = lax.dynamic_slice_in_dim(key_padded[height], first_row, 3 * BLOCK, 0).astype(jnp.float32).reshape(3 * BLOCK, HEADS, HEAD_DIM)
            value_rows = lax.dynamic_slice_in_dim(value_padded[height], first_row, 3 * BLOCK, 0).astype(jnp.float32).reshape(3 * BLOCK, HEADS, HEAD_DIM)
            scores = jnp.einsum('qhd,khd->hqk', query_heads, key_rows) * scale + height * log_two
            level_blocks = block_total >> height
            valid_mask = (col_block == 1) | ((col_block == 0) & (coarse_no >= 1)) | ((col_block == 2) & (coarse_no + 1 < level_blocks))
            scores = jnp.where(valid_mask[None, None, :], scores, masked_score)
            score_list.append(scores)
            key_list.append(key_rows)
            value_list.append(value_rows)
            starts.append(first_row)
        largest = functools.reduce(jnp.maximum, [jnp.max(s, axis=-1) for s in score_list])
        totals = functools.reduce(jnp.add, [jnp.sum(jnp.exp(s - largest[..., None]), axis=-1) for s in score_list])
        log_total = largest + jnp.log(totals)
        output = jnp.zeros((BLOCK, HEADS, HEAD_DIM), jnp.float32)
        rounded_list = []
        for height in range(LEVELS):
            weights = jnp.exp(score_list[height] - log_total[..., None])
            rounded = lax.optimization_barrier(weights.astype(jnp.bfloat16)).astype(jnp.float32)
            rounded_list.append(rounded)
            output = output + jnp.einsum('hqk,khd->qhd', rounded, value_list[height])
        attended_block = output.reshape(BLOCK, feat_width).astype(jnp.bfloat16)
        row_dots = jnp.sum(grad_heads * attended_block.astype(jnp.float32).reshape(BLOCK, HEADS, HEAD_DIM), axis=-1).T
        grad_q = jnp.zeros((BLOCK, HEADS, HEAD_DIM), jnp.float32)
        new_k = list(acc_k)
        new_v = list(acc_v)
        for height in range(LEVELS):
            weights = jnp.exp(score_list[height] - log_total[..., None])
            grad_weights = jnp.einsum('qhd,khd->hqk', grad_heads, value_list[height])
            grad_scores = lax.optimization_barrier((weights * (grad_weights - row_dots[..., None]) * scale).astype(jnp.bfloat16)).astype(jnp.float32)
            grad_q = grad_q + jnp.einsum('hqk,khd->qhd', grad_scores, key_list[height])
            key_part = jnp.einsum('hqk,qhd->khd', grad_scores, query_heads).reshape(3 * BLOCK, feat_width)
            value_part = jnp.einsum('hqk,qhd->khd', rounded_list[height], grad_heads).reshape(3 * BLOCK, feat_width)
            old_k = lax.dynamic_slice_in_dim(new_k[height], starts[height], 3 * BLOCK, 0)
            old_v = lax.dynamic_slice_in_dim(new_v[height], starts[height], 3 * BLOCK, 0)
            new_k[height] = lax.dynamic_update_slice_in_dim(new_k[height], old_k + key_part, starts[height], 0)
            new_v[height] = lax.dynamic_update_slice_in_dim(new_v[height], old_v + value_part, starts[height], 0)
        grad_block = grad_q.reshape(BLOCK, feat_width).astype(jnp.bfloat16)
        return (new_k, new_v), (attended_block, grad_block)

    (acc_keys, acc_values), (attended_blocks, grad_blocks) = lax.scan(advance, (acc_keys, acc_values), jnp.arange(block_total, dtype=jnp.int32))
    attended = attended_blocks.reshape(SEQ_LEN, feat_width)
    grad_queries = grad_blocks.reshape(SEQ_LEN, feat_width)
    inner_k = [x[BLOCK:-BLOCK] for x in acc_keys]
    inner_v = [x[BLOCK:-BLOCK] for x in acc_values]
    for height in range(LEVELS - 1, 0, -1):
        inner_k[height - 1] = inner_k[height - 1] + jnp.repeat(inner_k[height], 2, axis=0) * 0.5
        inner_v[height - 1] = inner_v[height - 1] + jnp.repeat(inner_v[height], 2, axis=0) * 0.5
    return attended, grad_queries, inner_k[0].astype(jnp.bfloat16), inner_v[0].astype(jnp.bfloat16)
```

```python
import math

import jax
import jax.numpy as jnp
from jax import lax
from jax.experimental import pallas as pl
from jax.experimental.pallas import tpu as pltpu
from jax.sharding import PartitionSpec as P

HEADS = 16
HEAD_DIM = 128
BLOCK = 64
HALF = BLOCK // 2
CHUNKS = 8
EARLY = 2
LAG = 8

SIB_FINE = 2 * BLOCK
OUT_FINE = SIB_FINE + BLOCK
OWN_L1 = OUT_FINE + BLOCK
OWN_L2 = OWN_L1 + BLOCK
SIB_L1 = OWN_L2 + HALF
SIB_L2 = SIB_L1 + BLOCK
OUT_L1 = SIB_L2 + HALF
OUT_L2 = OUT_L1 + BLOCK
FAR_L2 = OUT_L2 + BLOCK
CAND = FAR_L2 + BLOCK
COARSE = BLOCK + HALF
BACK = BLOCK + COARSE + BLOCK
RET = BLOCK + HALF
RELAY_L1 = BLOCK
RELAY_L2 = 2 * BLOCK
RELAY = RELAY_L2 + HALF
STAGES = 14

masked_score = -1e30
MESH = pl.DeviceIdType.MESH


def nt(a, b):
    return lax.dot_general(a, b, (((1,), (1,)), ((), ())), preferred_element_type=jnp.float32)


def nn(a, b):
    return lax.dot_general(a, b, (((1,), (0,)), ((), ())), preferred_element_type=jnp.float32)


def tn(a, b):
    return lax.dot_general(a, b, (((0,), (0,)), ((), ())), preferred_element_type=jnp.float32)


def pool_matrix(rows):
    row = lax.broadcasted_iota(jnp.int32, (rows // 2, rows), 0)
    col = lax.broadcasted_iota(jnp.int32, (rows // 2, rows), 1)
    return jnp.where((col >> 1) == row, 0.5, 0.0).astype(jnp.bfloat16)


def pooled(rows):
    return nn(pool_matrix(rows.shape[0]), rows).astype(jnp.bfloat16)


def spread_matrix(shape, row0, col0, rows, shift):
    row = lax.broadcasted_iota(jnp.int32, shape, 0) - row0
    col = lax.broadcasted_iota(jnp.int32, shape, 1) - col0
    hit = (row >= 0) & (row < rows) & ((row >> shift) == col)
    return jnp.where(hit, 0.5 ** shift, 0.0)


def spread(matrix, grads):
    matrix = matrix.astype(jnp.bfloat16)
    high = grads.astype(jnp.bfloat16)
    low = (grads - high.astype(jnp.float32)).astype(jnp.bfloat16)
    return nn(jnp.concatenate([matrix, matrix], axis=1), jnp.concatenate([high, low], axis=0))


def message_matrix():
    shape = (RET, BLOCK)
    return (spread_matrix(shape, 0, 0, BLOCK, 1)
            + spread_matrix(shape, 0, HALF, BLOCK, 2)
            + spread_matrix(shape, BLOCK, HALF + HALF // 2, HALF, 1))


def coarse_matrix():
    shape = (RET, HALF)
    return (spread_matrix(shape, 0, 0, BLOCK, 2)
            + spread_matrix(shape, BLOCK, HALF // 2, HALF, 1)).astype(jnp.bfloat16)


def own_matrix():
    shape = (2 * BLOCK, COARSE)
    return (spread_matrix(shape, 0, 0, 2 * BLOCK, 1)
            + spread_matrix(shape, 0, BLOCK, 2 * BLOCK, 2))


def kernel(q_ref, k_ref, v_ref, do_ref, att_ref, gq_ref, gk_ref, gv_ref,
           kv, grad, bias, relay, back_out, back_in, z_out, z_in, s_out, s_in,
           ret_out, ret_in, send_sem, recv_sem):
    count = lax.axis_size("seq")
    me = lax.axis_index("seq")
    side = lax.rem(me, 2)
    chip = me // 2
    odd = lax.rem(chip, 2)
    sib = me + 1 - 2 * side
    is_p = lax.rem(side + chip, 2) == 1
    is_d = jnp.logical_not(is_p)
    peer = 2 * (chip + 1 - 2 * odd) + 1 - side
    step = 4 - 8 * odd
    has_next = (me + step >= 0) & (me + step < count)
    has_prev = (me - step >= 0) & (me - step < count)
    has_outer = is_p | has_prev
    has_far = is_d | has_prev
    d_next = is_d & has_next
    d_prev = is_d & has_prev
    p_next = is_p & has_next
    feat = q_ref.shape[1]
    width = feat // CHUNKS
    scale = HEAD_DIM ** -0.5
    inner_start = pl.multiple_of(BLOCK * (1 - side), BLOCK)
    outer_start = pl.multiple_of(BLOCK * side, BLOCK)
    inner_half = pl.multiple_of(HALF * (1 - side), HALF)

    barrier = pltpu.get_barrier_semaphore()

    def greet(target):
        pl.semaphore_signal(barrier, inc=1, device_id={"seq": target}, device_id_type=MESH)

    greet(sib)
    greet(peer)

    @pl.when(d_next)
    def _():
        greet(me + step)

    @pl.when(p_next)
    def _():
        greet(sib + step)

    @pl.when(d_prev)
    def _():
        greet(me - step)
        greet(sib - step)

    own = pl.ds(0, 2 * BLOCK)
    for which, ref in enumerate((k_ref, v_ref)):
        kv[which, own, :] = ref[...]

    @pl.when(jnp.logical_not(has_outer))
    def _():
        for which in range(2):
            kv[which, OUT_FINE:OUT_FINE + BLOCK, :] = jnp.zeros((BLOCK, feat), jnp.bfloat16)
            kv[which, OUT_L1:OUT_L1 + 2 * BLOCK, :] = jnp.zeros((2 * BLOCK, feat), jnp.bfloat16)

    @pl.when(is_d & jnp.logical_not(has_next))
    def _():
        z_in[:, 0:RET, :] = jnp.zeros((2, RET, feat), jnp.bfloat16)

    lane = lax.broadcasted_iota(jnp.int32, (BLOCK, 2 * BLOCK), 1)
    is_outer_lane = (lane >> 6) == side
    zero = jnp.zeros((BLOCK, 2 * BLOCK), jnp.float32)
    bias[0:BLOCK] = zero
    bias[BLOCK:2 * BLOCK] = zero
    bias[SIB_FINE:SIB_FINE + BLOCK] = jnp.where(is_outer_lane, masked_score, zero)
    bias[OUT_FINE:OUT_FINE + BLOCK] = jnp.where(is_outer_lane & has_outer, zero, masked_score)
    bias[OWN_L1:OWN_L1 + BLOCK] = zero + 1.0
    bias[OWN_L2:OWN_L2 + HALF] = zero[:HALF] + 2.0
    bias[SIB_L1:SIB_L1 + BLOCK] = zero + 1.0
    bias[SIB_L2:SIB_L2 + HALF] = zero[:HALF] + 2.0
    bias[OUT_L1:OUT_L1 + BLOCK] = jnp.where(has_outer, zero + 1.0, masked_score)
    bias[OUT_L2:OUT_L2 + BLOCK] = jnp.where(has_outer, zero + 2.0, masked_score)
    bias[FAR_L2:FAR_L2 + BLOCK] = jnp.where(has_far, zero + 2.0, masked_score)

    peers = 2 + has_next.astype(jnp.int32) + 2 * d_prev.astype(jnp.int32)
    pl.semaphore_wait(barrier, peers)

    def copy(stage, chunk, src, src_row, dst, dst_row, rows, target):
        cols = pl.ds(chunk * width, width)
        return pltpu.make_async_remote_copy(
            src_ref=src.at[:, pl.ds(src_row, rows), cols],
            dst_ref=dst.at[:, pl.ds(dst_row, rows), cols],
            send_sem=send_sem.at[stage, chunk],
            recv_sem=recv_sem.at[stage, chunk],
            device_id={"seq": target},
            device_id_type=MESH,
        )

    def sib_fine(g):
        return copy(0, g, kv, inner_start, kv, SIB_FINE, BLOCK, sib)

    def sib_coarse(g):
        return copy(1, g, kv, OWN_L1, kv, SIB_L1, COARSE, sib)

    def p_fine(g):
        return copy(2, g, kv, outer_start, kv, OUT_FINE, BLOCK, peer)

    def p_l1(g):
        return copy(3, g, kv, OWN_L1 + inner_half, kv, OUT_L1 + HALF, HALF, peer)

    def d_fine(g):
        return copy(2, g, kv, outer_start, relay, 0, BLOCK, peer)

    def d_l1(g):
        return copy(3, g, kv, OWN_L1 + inner_half, relay, RELAY_L1 + HALF, HALF, peer)

    def z_fine(g):
        return copy(4, g, relay, 0, kv, OUT_FINE, BLOCK, me + step)

    def z_l1(g):
        return copy(5, g, relay, RELAY_L1 + HALF, kv, OUT_L1 + HALF, HALF, me + step)

    def z_l2(g):
        return copy(6, g, kv, OUT_L2, kv, OUT_L2 + HALF, HALF, sib + step)

    def sib_l2(g):
        return copy(7, g, relay, RELAY_L2, kv, OUT_L2 + HALF, HALF, sib)

    def far(g):
        return copy(8, g, kv, OUT_L2, kv, FAR_L2, BLOCK, sib)

    def back(g):
        return copy(9, g, back_out, 0, back_in, 0, BACK, sib)

    def z_main(g):
        return copy(10, g, z_out, 0, z_in, 0, RET, me - step)

    def z_grad2(g):
        return copy(11, g, z_out, RET, z_in, RET, HALF, sib - step)

    def sib_grad2(g):
        return copy(12, g, s_out, 0, s_in, 0, HALF, sib)

    def ret(g):
        return copy(13, g, ret_out, 0, ret_in, 0, RET, peer)

    def start_fine(g):
        @pl.when(is_p)
        def _():
            p_fine(g).start()

        @pl.when(is_d)
        def _():
            d_fine(g).start()

    def start_l1(g):
        @pl.when(is_p)
        def _():
            p_l1(g).start()

        @pl.when(is_d)
        def _():
            d_l1(g).start()

    for g in range(EARLY):
        start_fine(g)
    for which in range(2):
        first = pooled(kv[which, own, :])
        kv[which, OWN_L1:OWN_L1 + BLOCK, :] = first
        kv[which, OWN_L2:OWN_L2 + HALF, :] = pooled(first)
    for g in range(CHUNKS):
        if g >= EARLY:
            start_fine(g)
        start_l1(g)
        sib_coarse(g).start()
        sib_fine(g).start()

    def derive(ref, which, cols, fine, first, second):
        ref[which, pl.ds(first, HALF), cols] = pooled(ref[which, pl.ds(fine, BLOCK), cols])
        ref[which, pl.ds(second, HALF), cols] = pooled(ref[which, pl.ds(first, BLOCK), cols])

    def forward(g):
        cols = pl.ds(g * width, width)

        @pl.when(is_p)
        def _():
            p_fine(g).wait_recv()
            p_l1(g).wait_recv()
            for which in range(2):
                derive(kv, which, cols, OUT_FINE, OUT_L1, OUT_L2)

        @pl.when(p_next)
        def _():
            z_l2(g).start()

        @pl.when(is_d)
        def _():
            d_fine(g).wait_recv()
            d_l1(g).wait_recv()

        @pl.when(d_next)
        def _():
            z_fine(g).start()
            z_l1(g).start()

        @pl.when(is_d)
        def _():
            for which in range(2):
                derive(relay, which, cols, 0, RELAY_L1, RELAY_L2)
            sib_l2(g).start()

    def share_far(g):
        cols = pl.ds(g * width, width)

        @pl.when(is_p)
        def _():
            sib_l2(g).wait_recv()

        @pl.when(d_prev)
        def _():
            z_fine(g).wait_recv()
            z_l1(g).wait_recv()
            for which in range(2):
                derive(kv, which, cols, OUT_FINE, OUT_L1, OUT_L2)
            z_l2(g).wait_recv()
        far(g).start()

    def store_parts(which, part, cols):
        for start, end in ((0, SIB_FINE), (OUT_FINE, SIB_L1), (OUT_L1, FAR_L2)):
            grad[which, start:end, cols] = part[start:end]
        for dst, src, rows in ((0, SIB_FINE, BLOCK), (BLOCK, SIB_L1, COARSE),
                               (BLOCK + COARSE, FAR_L2, BLOCK)):
            back_out[which, dst:dst + rows, cols] = part[src:src + rows].astype(jnp.bfloat16)

    def attend(first, number):
        def score(h):
            cols = pl.ds(h * HEAD_DIM, HEAD_DIM)
            scores = nt(kv[0, :, cols], q_ref[:, cols]) * (scale * math.log2(math.e)) + bias[...]
            grad_weights = nt(kv[1, :, cols], do_ref[:, cols])
            return scores, grad_weights, jnp.max(scores, axis=0, keepdims=True)

        def weigh(scores, grad_weights, largest):
            raised = jnp.exp2(scores - largest)
            weights = raised * (1.0 / jnp.sum(raised, axis=0, keepdims=True))
            row_dots = jnp.sum(weights * grad_weights, axis=0, keepdims=True)
            grad_scores = weights * ((grad_weights - row_dots) * scale)
            return weights.astype(jnp.bfloat16), grad_scores.astype(jnp.bfloat16)

        def combine(h, weights_b, grad_scores):
            cols = pl.ds(h * HEAD_DIM, HEAD_DIM)
            att_ref[:, cols] = tn(weights_b, kv[1, :, cols]).astype(jnp.bfloat16)
            store_parts(1, nn(weights_b, do_ref[:, cols]), cols)
            gq_ref[:, cols] = tn(grad_scores, kv[0, :, cols]).astype(jnp.bfloat16)
            store_parts(0, nn(grad_scores, q_ref[:, cols]), cols)

        fronts = [score(first + i) for i in range(number)]
        for i, front in enumerate(fronts):
            combine(first + i, *weigh(*front))

    def folded(which, cols):
        coarse = jnp.concatenate([grad[which, pl.ds(OUT_L1, HALF), cols],
                                  grad[which, pl.ds(OUT_L2, HALF), cols]], axis=0)
        total = spread(message_matrix(), coarse)
        total += jnp.concatenate([grad[which, pl.ds(OUT_FINE, BLOCK), cols],
                                  grad[which, pl.ds(OUT_L1 + HALF, HALF), cols]], axis=0)
        return total.astype(jnp.bfloat16)

    def send_outer(g):
        cols = pl.ds(g * width, width)
        back(g).wait_recv()
        for which in range(2):
            def take(row, rows):
                return back_in[which, pl.ds(row, rows), cols].astype(jnp.float32)
            rows = pl.ds(inner_start, BLOCK)
            grad[which, rows, cols] += take(0, BLOCK)
            rows = pl.ds(OWN_L1, COARSE)
            grad[which, rows, cols] += take(BLOCK, COARSE)
            rows = pl.ds(OUT_L2, BLOCK)
            grad[which, rows, cols] += take(BLOCK + COARSE, BLOCK)

        @pl.when(d_prev)
        def _():
            for which in range(2):
                z_out[which, pl.ds(0, RET), cols] = folded(which, cols)
                second = grad[which, pl.ds(OUT_L2 + HALF, HALF), cols]
                z_out[which, pl.ds(RET, HALF), cols] = second.astype(jnp.bfloat16)
            z_main(g).start()
            z_grad2(g).start()

        @pl.when(is_p)
        def _():
            for which in range(2):
                s_out[which, :, cols] = grad[which, pl.ds(OUT_L2 + HALF, HALF), cols].astype(jnp.bfloat16)
            sib_grad2(g).start()

    def send_peer(g):
        cols = pl.ds(g * width, width)

        @pl.when(p_next)
        def _():
            z_grad2(g).wait_recv()
            for which in range(2):
                grad[which, pl.ds(OUT_L2, HALF), cols] += (
                    z_in[which, pl.ds(RET, HALF), cols].astype(jnp.float32))

        @pl.when(is_p)
        def _():
            for which in range(2):
                ret_out[which, :, cols] = folded(which, cols)

        @pl.when(d_next)
        def _():
            z_main(g).wait_recv()

        @pl.when(is_d)
        def _():
            sib_grad2(g).wait_recv()
            for which in range(2):
                total = nn(coarse_matrix(), s_in[which, :, cols])
                total += z_in[which, pl.ds(0, RET), cols].astype(jnp.float32)
                ret_out[which, :, cols] = total.astype(jnp.bfloat16)
        ret(g).start()

    def finish(g):
        cols = pl.ds(g * width, width)
        ret(g).wait_recv()
        for which, ref in enumerate((gk_ref, gv_ref)):
            rows = pl.ds(outer_start, BLOCK)
            grad[which, rows, cols] += ret_in[which, pl.ds(0, BLOCK), cols].astype(jnp.float32)
            rows = pl.ds(OWN_L1 + inner_half, HALF)
            grad[which, rows, cols] += ret_in[which, pl.ds(BLOCK, HALF), cols].astype(jnp.float32)
            fine = grad[which, pl.ds(0, 2 * BLOCK), cols]
            fine += spread(own_matrix(), grad[which, pl.ds(OWN_L1, COARSE), cols])
            ref[:, cols] = fine.astype(jnp.bfloat16)

    heads = width // HEAD_DIM
    forward(0)
    for g in range(CHUNKS):
        if g + 1 < CHUNKS:
            forward(g + 1)
        share_far(g)
        sib_coarse(g).wait_recv()
        sib_fine(g).wait_recv()
        far(g).wait_recv()
        attend(g * heads, heads)
        back(g).start()
        if g > 0:
            send_outer(g - 1)
        if g > 1:
            send_peer(g - 2)
        if g >= LAG:
            finish(g - LAG)
    send_outer(CHUNKS - 1)
    for g in range(max(0, CHUNKS - 2), CHUNKS):
        send_peer(g)
    for g in range(max(0, CHUNKS - LAG), CHUNKS):
        finish(g)
    for g in range(CHUNKS):
        for item in (sib_fine, sib_coarse, p_fine, p_l1, far, back, ret):
            item(g).wait_send()

        @pl.when(is_p)
        def _():
            sib_grad2(g).wait_send()

        @pl.when(is_d)
        def _():
            sib_l2(g).wait_send()

        @pl.when(p_next)
        def _():
            z_l2(g).wait_send()

        @pl.when(d_next)
        def _():
            z_fine(g).wait_send()
            z_l1(g).wait_send()

        @pl.when(d_prev)
        def _():
            z_main(g).wait_send()
            z_grad2(g).wait_send()


def place(*refs):
    held, sems = refs[8:]
    loads = [pltpu.make_async_copy(refs[i], held.at[i], sems.at[0, i]) for i in range(4)]
    stores = [pltpu.make_async_copy(held.at[i], refs[4 + i], sems.at[1, i]) for i in range(4)]
    for item in loads:
        item.start()
    for load, store in zip(loads, stores):
        load.wait()
        store.start()
    for item in stores:
        item.wait()


def body(queries, key_input, value_input, cotangent):
    rows, feat = queries.shape
    out = jax.ShapeDtypeStruct((rows, feat), jnp.bfloat16)
    results = pl.pallas_call(
        kernel,
        name="hier_attention",
        out_shape=[out] * 4,
        in_specs=[pl.BlockSpec(memory_space=pltpu.VMEM)] * 4,
        out_specs=[pl.BlockSpec(memory_space=pltpu.VMEM)] * 4,
        scratch_shapes=[
            pltpu.VMEM((2, CAND, feat), jnp.bfloat16),
            pltpu.VMEM((2, CAND, feat), jnp.float32),
            pltpu.VMEM((CAND, rows), jnp.float32),
            pltpu.VMEM((2, RELAY, feat), jnp.bfloat16),
            pltpu.VMEM((2, BACK, feat), jnp.bfloat16),
            pltpu.VMEM((2, BACK, feat), jnp.bfloat16),
            pltpu.VMEM((2, RET + HALF, feat), jnp.bfloat16),
            pltpu.VMEM((2, RET + HALF, feat), jnp.bfloat16),
            pltpu.VMEM((2, HALF, feat), jnp.bfloat16),
            pltpu.VMEM((2, HALF, feat), jnp.bfloat16),
            pltpu.VMEM((2, RET, feat), jnp.bfloat16),
            pltpu.VMEM((2, RET, feat), jnp.bfloat16),
            pltpu.SemaphoreType.DMA((STAGES, CHUNKS)),
            pltpu.SemaphoreType.DMA((STAGES, CHUNKS)),
        ],
        compiler_params=pltpu.CompilerParams(
            collective_id=0, has_side_effects=True, vmem_limit_bytes=56 * 1024 * 1024),
    )(queries, key_input, value_input, cotangent)
    return tuple(pl.pallas_call(
        place,
        name="place",
        out_shape=[out] * 4,
        in_specs=[pl.BlockSpec(memory_space=pl.ANY)] * 4,
        out_specs=[pl.BlockSpec(memory_space=pl.ANY)] * 4,
        scratch_shapes=[pltpu.VMEM((4, rows, feat), jnp.bfloat16), pltpu.SemaphoreType.DMA((2, 4))],
    )(*results))


def solution(mesh):
    spec = P(("groups", "seq"), None)
    return jax.shard_map(
        body, mesh=mesh, in_specs=(spec,) * 4, out_specs=(spec,) * 4, check_vma=False)
```

```python
import math

import jax
import jax.numpy as jnp
from jax import lax
from jax.experimental import pallas as pl
from jax.experimental.pallas import tpu as pltpu
from jax.sharding import PartitionSpec as P

HEADS = 16
HEAD_DIM = 128
BLOCK = 64
HALF = BLOCK // 2
CHUNKS = 8
PIECES = 2
SHARE = 2
OUTER = 3
PEER = 5
LAST = 8

SIB_FINE = 2 * BLOCK
OWN_COARSE = SIB_FINE + BLOCK
OWN_L2 = OWN_COARSE + BLOCK
COARSE = BLOCK + HALF
SIB_COARSE = OWN_COARSE + COARSE
OUT = SIB_COARSE + COARSE
FAR = OUT + 3 * BLOCK
CAND = FAR + BLOCK
RELAY = CAND
KV_ROWS = RELAY + 2 * BLOCK + HALF
MESSAGE = BLOCK + HALF
DERIVED = MESSAGE
SECOND = DERIVED + HALF
G_COARSE = 2 * BLOCK
G_OUT = G_COARSE + COARSE
GRAD_ROWS = G_OUT + 3 * BLOCK
B_FAR = BLOCK + COARSE
BACK = B_FAR + BLOCK
IN_ROWS = BACK + MESSAGE
M_MESSAGE = 0
M_OWN = M_MESSAGE + MESSAGE
M_SECOND = M_OWN + 2 * BLOCK
M_POOL = M_SECOND + MESSAGE
M_ROWS = M_POOL + HALF
STAGES = 9

masked_score = -1e30
MESH = pl.DeviceIdType.MESH


def nt(a, b):
    return lax.dot_general(a, b, (((1,), (1,)), ((), ())), preferred_element_type=jnp.float32)


def nn(a, b):
    return lax.dot_general(a, b, (((1,), (0,)), ((), ())), preferred_element_type=jnp.float32)


def tn(a, b):
    return lax.dot_general(a, b, (((0,), (0,)), ((), ())), preferred_element_type=jnp.float32)


def pool_matrix(rows):
    row = lax.broadcasted_iota(jnp.int32, (rows // 2, rows), 0)
    col = lax.broadcasted_iota(jnp.int32, (rows // 2, rows), 1)
    return jnp.where((col >> 1) == row, 0.5, 0.0).astype(jnp.bfloat16)


def pooled(rows):
    return nn(pool_matrix(rows.shape[0]), rows).astype(jnp.bfloat16)


def spread_matrix(shape, row0, col0, rows, shift):
    row = lax.broadcasted_iota(jnp.int32, shape, 0) - row0
    col = lax.broadcasted_iota(jnp.int32, shape, 1) - col0
    hit = (row >= 0) & (row < rows) & ((row >> shift) == col)
    return jnp.where(hit, 0.5 ** shift, 0.0)


def message_matrix():
    shape = (MESSAGE, BLOCK)
    return (spread_matrix(shape, 0, 0, BLOCK, 1)
            + spread_matrix(shape, 0, HALF, BLOCK, 2)
            + spread_matrix(shape, BLOCK, HALF + HALF // 2, HALF, 1)).astype(jnp.bfloat16)


def second_matrix():
    shape = (MESSAGE, HALF)
    return (spread_matrix(shape, 0, 0, BLOCK, 2)
            + spread_matrix(shape, BLOCK, HALF // 2, HALF, 1)).astype(jnp.bfloat16)


def own_matrix():
    shape = (2 * BLOCK, COARSE)
    return (spread_matrix(shape, 0, 0, 2 * BLOCK, 1)
            + spread_matrix(shape, 0, BLOCK, 2 * BLOCK, 2)).astype(jnp.bfloat16)


def split(rows):
    high = rows.astype(jnp.bfloat16)
    return high, (rows - high.astype(jnp.float32)).astype(jnp.bfloat16)


def kernel(q_ref, k_ref, v_ref, do_ref, att_ref, gq_ref, gk_ref, gv_ref,
           kv, grad, bias, mats, back_out, arrived, pass_on, ret_out,
           sib_send, sib_recv, send_sem, recv_sem):
    count = lax.axis_size("seq")
    me = lax.axis_index("seq")
    side = lax.rem(me, 2)
    chip = me // 2
    odd = lax.rem(chip, 2)
    sib = me + 1 - 2 * side
    p_role = lax.rem(side + chip, 2)
    d_role = 1 - p_role
    is_p = p_role == 1
    is_d = p_role == 0
    peer = 2 * (chip + 1 - 2 * odd) + 1 - side
    step = 4 - 8 * odd
    has_next = (me + step >= 0) & (me + step < count)
    has_prev = (me - step >= 0) & (me - step < count)
    has_outer = is_p | has_prev
    has_far = is_d | has_prev
    d_next = is_d & has_next
    d_prev = is_d & has_prev
    p_next = is_p & has_next
    feat = q_ref.shape[1]
    width = feat // CHUNKS
    heads = width // HEAD_DIM
    scale = HEAD_DIM ** -0.5
    inner_start = pl.multiple_of(BLOCK * (1 - side), BLOCK)
    outer_start = pl.multiple_of(BLOCK * side, BLOCK)
    inner_half = pl.multiple_of(HALF * (1 - side), HALF)
    landing = pl.multiple_of(OUT + (RELAY - OUT) * d_role, BLOCK)
    other = pl.multiple_of(OUT + (RELAY - OUT) * p_role, BLOCK)
    top = pl.multiple_of(BACK * (1 - side), HALF)
    bottom = pl.multiple_of(BACK * side, HALF)

    barrier = pltpu.get_barrier_semaphore()

    def greet(target):
        pl.semaphore_signal(barrier, inc=1, device_id={"seq": target}, device_id_type=MESH)

    greet(sib)
    greet(peer)

    @pl.when(d_next)
    def _():
        greet(me + step)

    @pl.when(p_next)
    def _():
        greet(sib + step)

    @pl.when(d_prev)
    def _():
        greet(me - step)
        greet(sib - step)

    for which, ref in enumerate((k_ref, v_ref)):
        rows = ref[...]
        kv[which, 0:2 * BLOCK, :] = rows
        first = pooled(rows)
        kv[which, OWN_COARSE:OWN_COARSE + BLOCK, :] = first
        kv[which, OWN_L2:OWN_L2 + HALF, :] = pooled(first)

    peers = 2 + has_next.astype(jnp.int32) + 2 * d_prev.astype(jnp.int32)
    pl.semaphore_wait(barrier, peers)

    def remote(src, dst, sends, recvs, target):
        return pltpu.make_async_remote_copy(
            src_ref=src, dst_ref=dst, send_sem=sends, recv_sem=recvs,
            device_id={"seq": target}, device_id_type=MESH)

    def copy(stage, g, src, src_row, dst, dst_row, rows, target):
        cols = pl.ds(g * width, width)
        return remote(src.at[:, pl.ds(src_row, rows), cols], dst.at[:, pl.ds(dst_row, rows), cols],
                      send_sem.at[stage, g], recv_sem.at[stage, g], target)

    def sib_copy(kind, piece):
        cols = pl.ds(piece * (feat // PIECES), feat // PIECES)
        src, dst, rows = ((inner_start, SIB_FINE, BLOCK), (OWN_COARSE, SIB_COARSE, COARSE))[kind]
        return remote(kv.at[:, pl.ds(src, rows), cols], kv.at[:, pl.ds(dst, rows), cols],
                      sib_send.at[kind, piece], sib_recv.at[kind, piece], sib)

    def y_fine(g):
        return copy(0, g, kv, outer_start, kv, landing, BLOCK, peer)

    def y_half(g):
        return copy(1, g, kv, OWN_COARSE + inner_half, kv, landing + BLOCK, HALF, peer)

    def z_rows(g):
        return copy(2, g, kv, RELAY, kv, OUT, MESSAGE, me + step)

    def second(g):
        return copy(3, g, kv, landing + SECOND, kv, OUT + SECOND + HALF, HALF, sib + step * p_role)

    def far(g):
        return copy(4, g, kv, OUT + SECOND, kv, FAR, BLOCK, sib)

    def back(g):
        return copy(5, g, back_out, 0, arrived, 0, BACK, sib)

    def z_grads(g):
        return copy(6, g, pass_on.at[0], 0, pass_on.at[1], 0, MESSAGE, me - step)

    def second_grads(g):
        return copy(7, g, pass_on.at[0], MESSAGE, pass_on.at[1], MESSAGE, HALF, sib - step * d_role)

    def ret(g):
        return copy(8, g, ret_out, 0, arrived, BACK, MESSAGE, peer)

    sends_second = is_d | p_next
    gets_second = is_p | d_prev

    for g in range(CHUNKS):
        y_fine(g).start()
        y_half(g).start()
        if g == 0:
            for piece in range(PIECES):
                sib_copy(0, piece).start()
                sib_copy(1, piece).start()

    @pl.when(jnp.logical_not(has_outer))
    def _():
        kv[:, OUT:OUT + 3 * BLOCK, :] = jnp.zeros((2, 3 * BLOCK, feat), jnp.bfloat16)

    @pl.when(is_d & jnp.logical_not(has_next))
    def _():
        pass_on[1, :, 0:MESSAGE, :] = jnp.zeros((2, MESSAGE, feat), jnp.bfloat16)

    @pl.when(is_p & jnp.logical_not(has_next))
    def _():
        pass_on[1, :, MESSAGE:MESSAGE + HALF, :] = jnp.zeros((2, HALF, feat), jnp.bfloat16)

    lane = lax.broadcasted_iota(jnp.int32, (BLOCK, 2 * BLOCK), 1)
    is_outer_lane = (lane >> 6) == side
    zero = jnp.zeros((BLOCK, 2 * BLOCK), jnp.float32)
    for row in (0, BLOCK):
        bias[row:row + BLOCK] = zero
    bias[SIB_FINE:SIB_FINE + BLOCK] = jnp.where(is_outer_lane, masked_score, zero)
    for row in (OWN_COARSE, SIB_COARSE):
        bias[row:row + BLOCK] = zero + 1.0
        bias[row + BLOCK:row + COARSE] = zero[:HALF] + 2.0
    bias[OUT:OUT + BLOCK] = jnp.where(is_outer_lane & has_outer, zero, masked_score)
    bias[OUT + BLOCK:OUT + 2 * BLOCK] = jnp.where(has_outer, zero + 1.0, masked_score)
    bias[OUT + SECOND:OUT + 3 * BLOCK] = jnp.where(has_outer, zero + 2.0, masked_score)
    bias[FAR:FAR + BLOCK] = jnp.where(has_far, zero + 2.0, masked_score)

    message = message_matrix()
    mats[M_MESSAGE:M_MESSAGE + MESSAGE, 0:2 * BLOCK] = jnp.concatenate([message, message], axis=1)
    own = own_matrix()
    inner = spread_matrix((2 * BLOCK, HALF), inner_start, 0, BLOCK, 1).astype(jnp.bfloat16)
    mats[M_OWN:M_OWN + 2 * BLOCK, 0:2 * COARSE + HALF] = jnp.concatenate([own, inner, own], axis=1)
    mats[M_SECOND:M_SECOND + MESSAGE, 0:HALF] = second_matrix()
    mats[M_POOL:M_POOL + HALF, 0:BLOCK] = pool_matrix(BLOCK)

    def columns(g):
        return pl.ds(g * width, width)

    def derive(base, g):
        cols = columns(g)
        pool = mats[M_POOL:M_POOL + HALF, 0:BLOCK]
        for which in range(2):
            first = nn(pool, kv[which, pl.ds(base, BLOCK), cols]).astype(jnp.bfloat16)
            both = jnp.concatenate([first, kv[which, pl.ds(base + BLOCK, HALF), cols]], axis=0)
            kv[which, pl.ds(base + DERIVED, HALF), cols] = first
            kv[which, pl.ds(base + SECOND, HALF), cols] = nn(pool, both).astype(jnp.bfloat16)

    def store_parts(which, part, cols):
        for dst, src, rows in ((0, 0, 2 * BLOCK), (G_COARSE, OWN_COARSE, COARSE), (G_OUT, OUT, 3 * BLOCK)):
            grad[which, dst:dst + rows, cols] = part[src:src + rows]
        for dst, src, rows in ((0, SIB_FINE, BLOCK), (BLOCK, SIB_COARSE, COARSE), (B_FAR, FAR, BLOCK)):
            back_out[which, dst:dst + rows, cols] = part[src:src + rows].astype(jnp.bfloat16)

    def attend(first, number):
        def score(h):
            cols = pl.ds(h * HEAD_DIM, HEAD_DIM)
            scores = nt(kv[0, 0:CAND, cols], q_ref[:, cols]) * (scale * math.log2(math.e)) + bias[...]
            grad_weights = nt(kv[1, 0:CAND, cols], do_ref[:, cols])
            return scores, grad_weights, jnp.max(scores, axis=0, keepdims=True)

        def weigh(scores, grad_weights, largest):
            raised = jnp.exp2(scores - largest)
            weights = raised * (1.0 / jnp.sum(raised, axis=0, keepdims=True))
            row_dots = jnp.sum(weights * grad_weights, axis=0, keepdims=True)
            grad_scores = weights * ((grad_weights - row_dots) * scale)
            return weights.astype(jnp.bfloat16), grad_scores.astype(jnp.bfloat16)

        def combine(h, weights_b, grad_scores):
            cols = pl.ds(h * HEAD_DIM, HEAD_DIM)
            att_ref[:, cols] = tn(weights_b, kv[1, 0:CAND, cols]).astype(jnp.bfloat16)
            store_parts(1, nn(weights_b, do_ref[:, cols]), cols)
            gq_ref[:, cols] = tn(grad_scores, kv[0, 0:CAND, cols]).astype(jnp.bfloat16)
            store_parts(0, nn(grad_scores, q_ref[:, cols]), cols)

        fronts = [score(first + i) for i in range(number)]
        for i, front in enumerate(fronts):
            combine(first + i, *weigh(*front))

    def fold(g):
        cols = columns(g)
        matrix = mats[M_MESSAGE:M_MESSAGE + MESSAGE, 0:2 * BLOCK]
        for which in range(2):
            second = (grad[which, G_OUT + SECOND:GRAD_ROWS, cols]
                      + arrived[which, B_FAR:BACK, cols].astype(jnp.float32))
            coarse = jnp.concatenate([grad[which, G_OUT + DERIVED:G_OUT + SECOND, cols], second[:HALF]], axis=0)
            total = nn(matrix, jnp.concatenate(split(coarse), axis=0)) + grad[which, G_OUT:G_OUT + MESSAGE, cols]
            pass_on[0, which, 0:MESSAGE, cols] = total.astype(jnp.bfloat16)
            pass_on[0, which, MESSAGE:MESSAGE + HALF, cols] = second[HALF:].astype(jnp.bfloat16)

    def gather(g):
        cols = columns(g)
        matrix = mats[M_SECOND:M_SECOND + MESSAGE, 0:HALF]
        for which in range(2):
            total = nn(matrix, pass_on[1, which, MESSAGE:MESSAGE + HALF, cols])
            total += pass_on[d_role, which, 0:MESSAGE, cols].astype(jnp.float32)
            ret_out[which, :, cols] = total.astype(jnp.bfloat16)

    def finish(g):
        cols = columns(g)
        matrix = mats[M_OWN:M_OWN + 2 * BLOCK, 0:2 * COARSE + HALF]
        for which, ref in enumerate((gk_ref, gv_ref)):
            coarse = (grad[which, G_COARSE:G_OUT, cols]
                      + arrived[which, BLOCK:BLOCK + COARSE, cols].astype(jnp.float32))
            high, low = split(coarse)
            parts = jnp.concatenate([high, arrived[which, BACK + BLOCK:IN_ROWS, cols], low], axis=0)
            fine = jnp.concatenate([arrived[which, pl.ds(top, BLOCK), cols],
                                    arrived[which, pl.ds(bottom, BLOCK), cols]], axis=0)
            total = nn(matrix, parts) + (grad[which, 0:2 * BLOCK, cols] + fine.astype(jnp.float32))
            ref[:, cols] = total.astype(jnp.bfloat16)

    def when(cond, item, act):
        @pl.when(cond)
        def _():
            getattr(item, act)()

    for i in range(CHUNKS + LAST):
        def now(lag):
            return 0 <= i - lag < CHUNKS

        if now(0):
            y_fine(i).wait_recv()
            y_half(i).wait_recv()
            when(d_next, z_rows(i), "start")
        if now(SHARE):
            when(d_prev, z_rows(i - SHARE), "wait_recv")
            when(gets_second, second(i - SHARE), "wait_recv")
        if now(0):
            derive(landing, i)
        if now(SHARE):
            derive(other, i - SHARE)
            far(i - SHARE).start()
        if now(0):
            when(sends_second, second(i), "start")
        if now(OUTER):
            back(i - OUTER).wait_recv()
            fold(i - OUTER)
            when(d_prev, z_grads(i - OUTER), "start")
            when(gets_second, second_grads(i - OUTER), "start")
        if now(PEER):
            when(d_next, z_grads(i - PEER), "wait_recv")
            when(sends_second, second_grads(i - PEER), "wait_recv")
            gather(i - PEER)
            ret(i - PEER).start()
        if now(SHARE):
            g = i - SHARE
            if g % (CHUNKS // PIECES) == 0:
                for kind in range(2):
                    sib_copy(kind, g // (CHUNKS // PIECES)).wait_recv()
            far(g).wait_recv()
            attend(g * heads, heads)
            back(g).start()
        if now(LAST):
            ret(i - LAST).wait_recv()
            finish(i - LAST)

    for piece in range(PIECES):
        for kind in range(2):
            sib_copy(kind, piece).wait_send()
    for g in range(CHUNKS):
        for item in (y_fine, y_half, far, back, ret):
            item(g).wait_send()
        when(sends_second, second(g), "wait_send")
        when(d_next, z_rows(g), "wait_send")
        when(d_prev, z_grads(g), "wait_send")
        when(gets_second, second_grads(g), "wait_send")


def place(*refs):
    held, sems = refs[8:]
    loads = [pltpu.make_async_copy(refs[i], held.at[i], sems.at[0, i]) for i in range(4)]
    stores = [pltpu.make_async_copy(held.at[i], refs[4 + i], sems.at[1, i]) for i in range(4)]
    for item in loads:
        item.start()
    for load, store in zip(loads, stores):
        load.wait()
        store.start()
    for item in stores:
        item.wait()


def body(queries, key_input, value_input, cotangent):
    rows, feat = queries.shape
    out = jax.ShapeDtypeStruct((rows, feat), jnp.bfloat16)
    results = pl.pallas_call(
        kernel,
        name="hier_attention",
        out_shape=[out] * 4,
        in_specs=[pl.BlockSpec(memory_space=pltpu.VMEM)] * 4,
        out_specs=[pl.BlockSpec(memory_space=pltpu.VMEM)] * 4,
        scratch_shapes=[
            pltpu.VMEM((2, KV_ROWS, feat), jnp.bfloat16),
            pltpu.VMEM((2, GRAD_ROWS, feat), jnp.float32),
            pltpu.VMEM((CAND, rows), jnp.float32),
            pltpu.VMEM((M_ROWS, 2 * rows), jnp.bfloat16),
            pltpu.VMEM((2, BACK, feat), jnp.bfloat16),
            pltpu.VMEM((2, IN_ROWS, feat), jnp.bfloat16),
            pltpu.VMEM((2, 2, MESSAGE + HALF, feat), jnp.bfloat16),
            pltpu.VMEM((2, MESSAGE, feat), jnp.bfloat16),
            pltpu.SemaphoreType.DMA((2, PIECES)),
            pltpu.SemaphoreType.DMA((2, PIECES)),
            pltpu.SemaphoreType.DMA((STAGES, CHUNKS)),
            pltpu.SemaphoreType.DMA((STAGES, CHUNKS)),
        ],
        compiler_params=pltpu.CompilerParams(
            collective_id=0, has_side_effects=True, vmem_limit_bytes=56 * 1024 * 1024),
    )(queries, key_input, value_input, cotangent)
    return tuple(pl.pallas_call(
        place,
        name="place",
        out_shape=[out] * 4,
        in_specs=[pl.BlockSpec(memory_space=pl.ANY)] * 4,
        out_specs=[pl.BlockSpec(memory_space=pl.ANY)] * 4,
        scratch_shapes=[pltpu.VMEM((4, rows, feat), jnp.bfloat16), pltpu.SemaphoreType.DMA((2, 4))],
    )(*results))


def solution(mesh):
    spec = P(("groups", "seq"), None)
    return jax.shard_map(
        body, mesh=mesh, in_specs=(spec,) * 4, out_specs=(spec,) * 4, check_vma=False)
```

```python
import math

import jax
import jax.numpy as jnp
from jax import lax
from jax.experimental import pallas as pl
from jax.experimental.pallas import tpu as pltpu
from jax.sharding import PartitionSpec as P

HEADS = 16
HEAD_DIM = 128
BLOCK = 64
HALF = BLOCK // 2
CHUNKS = 8
EARLY = 2
PIECES = 2
SHARE = 2
OUTER = 3
PEER = 5
LAST = 8

SIB_FINE = 2 * BLOCK
OWN_COARSE = SIB_FINE + BLOCK
OWN_L2 = OWN_COARSE + BLOCK
COARSE = BLOCK + HALF
SIB_COARSE = OWN_COARSE + COARSE
OUT = SIB_COARSE + COARSE
FAR = OUT + 3 * BLOCK
CAND = FAR + BLOCK
RELAY = CAND
KV_ROWS = RELAY + 2 * BLOCK + HALF
MESSAGE = BLOCK + HALF
DERIVED = MESSAGE
SECOND = DERIVED + HALF
G_COARSE = 2 * BLOCK
G_OUT = G_COARSE + COARSE
GRAD_ROWS = G_OUT + 3 * BLOCK
B_FAR = BLOCK + COARSE
BACK = B_FAR + BLOCK
IN_ROWS = BACK + MESSAGE
M_MESSAGE = 0
M_OWN = M_MESSAGE + MESSAGE
M_SECOND = M_OWN + 2 * BLOCK
M_POOL = M_SECOND + MESSAGE
M_ROWS = M_POOL + HALF
STAGES = 9

masked_score = -1e30
MESH = pl.DeviceIdType.MESH


def nt(a, b):
    return lax.dot_general(a, b, (((1,), (1,)), ((), ())), preferred_element_type=jnp.float32)


def nn(a, b):
    return lax.dot_general(a, b, (((1,), (0,)), ((), ())), preferred_element_type=jnp.float32)


def tn(a, b):
    return lax.dot_general(a, b, (((0,), (0,)), ((), ())), preferred_element_type=jnp.float32)


def pool_matrix(rows):
    row = lax.broadcasted_iota(jnp.int32, (rows // 2, rows), 0)
    col = lax.broadcasted_iota(jnp.int32, (rows // 2, rows), 1)
    return jnp.where((col >> 1) == row, 0.5, 0.0).astype(jnp.bfloat16)


def pooled(rows):
    return nn(pool_matrix(rows.shape[0]), rows).astype(jnp.bfloat16)


def spread_matrix(shape, row0, col0, rows, shift):
    row = lax.broadcasted_iota(jnp.int32, shape, 0) - row0
    col = lax.broadcasted_iota(jnp.int32, shape, 1) - col0
    hit = (row >= 0) & (row < rows) & ((row >> shift) == col)
    return jnp.where(hit, 0.5 ** shift, 0.0)


def message_matrix():
    shape = (MESSAGE, BLOCK)
    return (spread_matrix(shape, 0, 0, BLOCK, 1)
            + spread_matrix(shape, 0, HALF, BLOCK, 2)
            + spread_matrix(shape, BLOCK, HALF + HALF // 2, HALF, 1)).astype(jnp.bfloat16)


def second_matrix():
    shape = (MESSAGE, HALF)
    return (spread_matrix(shape, 0, 0, BLOCK, 2)
            + spread_matrix(shape, BLOCK, HALF // 2, HALF, 1)).astype(jnp.bfloat16)


def own_matrix():
    shape = (2 * BLOCK, COARSE)
    return (spread_matrix(shape, 0, 0, 2 * BLOCK, 1)
            + spread_matrix(shape, 0, BLOCK, 2 * BLOCK, 2)).astype(jnp.bfloat16)


def split(rows):
    high = rows.astype(jnp.bfloat16)
    return high, (rows - high.astype(jnp.float32)).astype(jnp.bfloat16)


def kernel(queries, keys, values, cotangent, att_ref, gq_ref, gk_ref, gv_ref,
           q_ref, do_ref, kv, grad, bias, mats, back_out, arrived, pass_on, ret_out,
           load_sem, sib_send, sib_recv, send_sem, recv_sem):
    count = lax.axis_size("seq")
    me = lax.axis_index("seq")
    side = lax.rem(me, 2)
    chip = me // 2
    odd = lax.rem(chip, 2)
    sib = me + 1 - 2 * side
    p_role = lax.rem(side + chip, 2)
    d_role = 1 - p_role
    is_p = p_role == 1
    is_d = p_role == 0
    peer = 2 * (chip + 1 - 2 * odd) + 1 - side
    step = 4 - 8 * odd
    has_next = (me + step >= 0) & (me + step < count)
    has_prev = (me - step >= 0) & (me - step < count)
    has_outer = is_p | has_prev
    has_far = is_d | has_prev
    d_next = is_d & has_next
    d_prev = is_d & has_prev
    p_next = is_p & has_next
    feat = queries.shape[1]
    width = feat // CHUNKS
    heads = width // HEAD_DIM
    scale = HEAD_DIM ** -0.5
    inner_start = pl.multiple_of(BLOCK * (1 - side), BLOCK)
    outer_start = pl.multiple_of(BLOCK * side, BLOCK)
    inner_half = pl.multiple_of(HALF * (1 - side), HALF)
    landing = pl.multiple_of(OUT + (RELAY - OUT) * d_role, BLOCK)
    other = pl.multiple_of(OUT + (RELAY - OUT) * p_role, BLOCK)
    top = pl.multiple_of(BACK * (1 - side), HALF)
    bottom = pl.multiple_of(BACK * side, HALF)

    loads = [pltpu.make_async_copy(src, dst, load_sem.at[i]) for i, (src, dst) in enumerate((
        (keys, kv.at[0, 0:2 * BLOCK]), (values, kv.at[1, 0:2 * BLOCK]), (queries, q_ref), (cotangent, do_ref)))]
    for item in loads:
        item.start()

    barrier = pltpu.get_barrier_semaphore()

    def greet(target):
        pl.semaphore_signal(barrier, inc=1, device_id={"seq": target}, device_id_type=MESH)

    greet(sib)
    greet(peer)

    @pl.when(d_next)
    def _():
        greet(me + step)

    @pl.when(p_next)
    def _():
        greet(sib + step)

    @pl.when(d_prev)
    def _():
        greet(me - step)
        greet(sib - step)

    def pool_own(first, number):
        cols = pl.ds(first * width, number * width)
        for which in range(2):
            half = pooled(kv[which, 0:2 * BLOCK, cols])
            kv[which, OWN_COARSE:OWN_COARSE + BLOCK, cols] = half
            kv[which, OWN_L2:OWN_L2 + HALF, cols] = pooled(half)

    loads[0].wait()
    loads[1].wait()
    pool_own(0, EARLY)

    peers = 2 + has_next.astype(jnp.int32) + 2 * d_prev.astype(jnp.int32)
    pl.semaphore_wait(barrier, peers)

    def remote(src, dst, sends, recvs, target):
        return pltpu.make_async_remote_copy(
            src_ref=src, dst_ref=dst, send_sem=sends, recv_sem=recvs,
            device_id={"seq": target}, device_id_type=MESH)

    def copy(stage, g, src, src_row, dst, dst_row, rows, target):
        cols = pl.ds(g * width, width)
        return remote(src.at[:, pl.ds(src_row, rows), cols], dst.at[:, pl.ds(dst_row, rows), cols],
                      send_sem.at[stage, g], recv_sem.at[stage, g], target)

    def sib_copy(kind, piece):
        cols = pl.ds(piece * (feat // PIECES), feat // PIECES)
        src, dst, rows = ((inner_start, SIB_FINE, BLOCK), (OWN_COARSE, SIB_COARSE, COARSE))[kind]
        return remote(kv.at[:, pl.ds(src, rows), cols], kv.at[:, pl.ds(dst, rows), cols],
                      sib_send.at[kind, piece], sib_recv.at[kind, piece], sib)

    def y_fine(g):
        return copy(0, g, kv, outer_start, kv, landing, BLOCK, peer)

    def y_half(g):
        return copy(1, g, kv, OWN_COARSE + inner_half, kv, landing + BLOCK, HALF, peer)

    def z_rows(g):
        return copy(2, g, kv, RELAY, kv, OUT, MESSAGE, me + step)

    def second(g):
        return copy(3, g, kv, landing + SECOND, kv, OUT + SECOND + HALF, HALF, sib + step * p_role)

    def far(g):
        return copy(4, g, kv, OUT + SECOND, kv, FAR, BLOCK, sib)

    def back(g):
        return copy(5, g, back_out, 0, arrived, 0, BACK, sib)

    def z_grads(g):
        return copy(6, g, pass_on.at[0], 0, pass_on.at[1], 0, MESSAGE, me - step)

    def second_grads(g):
        return copy(7, g, pass_on.at[0], MESSAGE, pass_on.at[1], MESSAGE, HALF, sib - step * d_role)

    def ret(g):
        return copy(8, g, ret_out, 0, arrived, BACK, MESSAGE, peer)

    sends_second = is_d | p_next
    gets_second = is_p | d_prev

    for g in range(CHUNKS):
        if g == EARLY:
            pool_own(EARLY, CHUNKS - EARLY)
        if g < EARLY:
            y_fine(g).start()
        y_half(g).start()
        if EARLY <= g + 1 < CHUNKS:
            y_fine(g + 1).start()
    for piece in range(PIECES):
        sib_copy(0, piece).start()
        sib_copy(1, piece).start()

    @pl.when(jnp.logical_not(has_outer))
    def _():
        kv[:, OUT:OUT + 3 * BLOCK, :] = jnp.zeros((2, 3 * BLOCK, feat), jnp.bfloat16)

    @pl.when(is_d & jnp.logical_not(has_next))
    def _():
        pass_on[1, :, 0:MESSAGE, :] = jnp.zeros((2, MESSAGE, feat), jnp.bfloat16)

    @pl.when(is_p & jnp.logical_not(has_next))
    def _():
        pass_on[1, :, MESSAGE:MESSAGE + HALF, :] = jnp.zeros((2, HALF, feat), jnp.bfloat16)

    lane = lax.broadcasted_iota(jnp.int32, (BLOCK, 2 * BLOCK), 1)
    is_outer_lane = (lane >> 6) == side
    zero = jnp.zeros((BLOCK, 2 * BLOCK), jnp.float32)
    for row in (0, BLOCK):
        bias[row:row + BLOCK] = zero
    bias[SIB_FINE:SIB_FINE + BLOCK] = jnp.where(is_outer_lane, masked_score, zero)
    for row in (OWN_COARSE, SIB_COARSE):
        bias[row:row + BLOCK] = zero + 1.0
        bias[row + BLOCK:row + COARSE] = zero[:HALF] + 2.0
    bias[OUT:OUT + BLOCK] = jnp.where(is_outer_lane & has_outer, zero, masked_score)
    bias[OUT + BLOCK:OUT + 2 * BLOCK] = jnp.where(has_outer, zero + 1.0, masked_score)
    bias[OUT + SECOND:OUT + 3 * BLOCK] = jnp.where(has_outer, zero + 2.0, masked_score)
    bias[FAR:FAR + BLOCK] = jnp.where(has_far, zero + 2.0, masked_score)

    message = message_matrix()
    mats[M_MESSAGE:M_MESSAGE + MESSAGE, 0:2 * BLOCK] = jnp.concatenate([message, message], axis=1)
    own = own_matrix()
    inner = spread_matrix((2 * BLOCK, HALF), inner_start, 0, BLOCK, 1).astype(jnp.bfloat16)
    mats[M_OWN:M_OWN + 2 * BLOCK, 0:2 * COARSE + HALF] = jnp.concatenate([own, inner, own], axis=1)
    mats[M_SECOND:M_SECOND + MESSAGE, 0:HALF] = second_matrix()
    mats[M_POOL:M_POOL + HALF, 0:BLOCK] = pool_matrix(BLOCK)

    def columns(g):
        return pl.ds(g * width, width)

    def derive(base, g):
        cols = columns(g)
        pool = mats[M_POOL:M_POOL + HALF, 0:BLOCK]
        for which in range(2):
            first = nn(pool, kv[which, pl.ds(base, BLOCK), cols]).astype(jnp.bfloat16)
            both = jnp.concatenate([first, kv[which, pl.ds(base + BLOCK, HALF), cols]], axis=0)
            kv[which, pl.ds(base + DERIVED, HALF), cols] = first
            kv[which, pl.ds(base + SECOND, HALF), cols] = nn(pool, both).astype(jnp.bfloat16)

    def store_parts(which, part, cols):
        for dst, src, rows in ((0, 0, 2 * BLOCK), (G_COARSE, OWN_COARSE, COARSE), (G_OUT, OUT, 3 * BLOCK)):
            grad[which, dst:dst + rows, cols] = part[src:src + rows]
        for dst, src, rows in ((0, SIB_FINE, BLOCK), (BLOCK, SIB_COARSE, COARSE), (B_FAR, FAR, BLOCK)):
            back_out[which, dst:dst + rows, cols] = part[src:src + rows].astype(jnp.bfloat16)

    def attend(first, number):
        def score(h):
            cols = pl.ds(h * HEAD_DIM, HEAD_DIM)
            scores = nt(kv[0, 0:CAND, cols], q_ref[:, cols]) * (scale * math.log2(math.e)) + bias[...]
            grad_weights = nt(kv[1, 0:CAND, cols], do_ref[:, cols])
            return scores, grad_weights, jnp.max(scores, axis=0, keepdims=True)

        def weigh(scores, grad_weights, largest):
            raised = jnp.exp2(scores - largest)
            weights = raised * (1.0 / jnp.sum(raised, axis=0, keepdims=True))
            row_dots = jnp.sum(weights * grad_weights, axis=0, keepdims=True)
            grad_scores = weights * ((grad_weights - row_dots) * scale)
            return weights.astype(jnp.bfloat16), grad_scores.astype(jnp.bfloat16)

        def combine(h, weights_b, grad_scores):
            cols = pl.ds(h * HEAD_DIM, HEAD_DIM)
            att_ref[:, cols] = tn(weights_b, kv[1, 0:CAND, cols]).astype(jnp.bfloat16)
            store_parts(1, nn(weights_b, do_ref[:, cols]), cols)
            gq_ref[:, cols] = tn(grad_scores, kv[0, 0:CAND, cols]).astype(jnp.bfloat16)
            store_parts(0, nn(grad_scores, q_ref[:, cols]), cols)

        fronts = [score(first + i) for i in range(number)]
        for i, front in enumerate(fronts):
            combine(first + i, *weigh(*front))

    def fold(g):
        cols = columns(g)
        matrix = mats[M_MESSAGE:M_MESSAGE + MESSAGE, 0:2 * BLOCK]
        for which in range(2):
            second = (grad[which, G_OUT + SECOND:GRAD_ROWS, cols]
                      + arrived[which, B_FAR:BACK, cols].astype(jnp.float32))
            coarse = jnp.concatenate([grad[which, G_OUT + DERIVED:G_OUT + SECOND, cols], second[:HALF]], axis=0)
            total = nn(matrix, jnp.concatenate(split(coarse), axis=0)) + grad[which, G_OUT:G_OUT + MESSAGE, cols]
            pass_on[0, which, 0:MESSAGE, cols] = total.astype(jnp.bfloat16)
            pass_on[0, which, MESSAGE:MESSAGE + HALF, cols] = second[HALF:].astype(jnp.bfloat16)

    def gather(g):
        cols = columns(g)
        matrix = mats[M_SECOND:M_SECOND + MESSAGE, 0:HALF]
        for which in range(2):
            total = nn(matrix, pass_on[1, which, MESSAGE:MESSAGE + HALF, cols])
            total += pass_on[d_role, which, 0:MESSAGE, cols].astype(jnp.float32)
            ret_out[which, :, cols] = total.astype(jnp.bfloat16)

    def finish(g):
        cols = columns(g)
        matrix = mats[M_OWN:M_OWN + 2 * BLOCK, 0:2 * COARSE + HALF]
        for which, ref in enumerate((gk_ref, gv_ref)):
            coarse = (grad[which, G_COARSE:G_OUT, cols]
                      + arrived[which, BLOCK:BLOCK + COARSE, cols].astype(jnp.float32))
            high, low = split(coarse)
            parts = jnp.concatenate([high, arrived[which, BACK + BLOCK:IN_ROWS, cols], low], axis=0)
            fine = jnp.concatenate([arrived[which, pl.ds(top, BLOCK), cols],
                                    arrived[which, pl.ds(bottom, BLOCK), cols]], axis=0)
            total = nn(matrix, parts) + (grad[which, 0:2 * BLOCK, cols] + fine.astype(jnp.float32))
            ref[:, cols] = total.astype(jnp.bfloat16)

    def when(cond, item, act):
        @pl.when(cond)
        def _():
            getattr(item, act)()

    loads[2].wait()
    loads[3].wait()
    for i in range(CHUNKS + LAST):
        def now(lag):
            return 0 <= i - lag < CHUNKS

        if now(0):
            y_fine(i).wait_recv()
            y_half(i).wait_recv()
            when(d_next, z_rows(i), "start")
        if now(SHARE):
            when(d_prev, z_rows(i - SHARE), "wait_recv")
            when(gets_second, second(i - SHARE), "wait_recv")
        if now(0):
            derive(landing, i)
        if now(SHARE):
            derive(other, i - SHARE)
            far(i - SHARE).start()
        if now(0):
            when(sends_second, second(i), "start")
        if now(OUTER):
            back(i - OUTER).wait_recv()
            fold(i - OUTER)
            when(d_prev, z_grads(i - OUTER), "start")
            when(gets_second, second_grads(i - OUTER), "start")
        if now(PEER):
            when(d_next, z_grads(i - PEER), "wait_recv")
            when(sends_second, second_grads(i - PEER), "wait_recv")
            gather(i - PEER)
            ret(i - PEER).start()
        if now(SHARE):
            g = i - SHARE
            if g % (CHUNKS // PIECES) == 0:
                for kind in range(2):
                    sib_copy(kind, g // (CHUNKS // PIECES)).wait_recv()
            far(g).wait_recv()
            attend(g * heads, heads)
            back(g).start()
        if now(LAST):
            ret(i - LAST).wait_recv()
            finish(i - LAST)

    for piece in range(PIECES):
        for kind in range(2):
            sib_copy(kind, piece).wait_send()
    for g in range(CHUNKS):
        for item in (y_fine, y_half, far, back, ret):
            item(g).wait_send()
        when(sends_second, second(g), "wait_send")
        when(d_next, z_rows(g), "wait_send")
        when(d_prev, z_grads(g), "wait_send")
        when(gets_second, second_grads(g), "wait_send")


def place(*refs):
    sems = refs[8]
    stores = [pltpu.make_async_copy(refs[i], refs[4 + i], sems.at[i]) for i in range(4)]
    for item in stores:
        item.start()
    for item in stores:
        item.wait()


def body(queries, key_input, value_input, cotangent):
    rows, feat = queries.shape
    out = jax.ShapeDtypeStruct((rows, feat), jnp.bfloat16)
    results = pl.pallas_call(
        kernel,
        name="hier_attention",
        out_shape=[pltpu.VMEM((rows, feat), jnp.bfloat16)] * 4,
        in_specs=[pl.BlockSpec(memory_space=pl.ANY)] * 4,
        out_specs=[pl.BlockSpec(memory_space=pltpu.VMEM)] * 4,
        scratch_shapes=[
            pltpu.VMEM((rows, feat), jnp.bfloat16),
            pltpu.VMEM((rows, feat), jnp.bfloat16),
            pltpu.VMEM((2, KV_ROWS, feat), jnp.bfloat16),
            pltpu.VMEM((2, GRAD_ROWS, feat), jnp.float32),
            pltpu.VMEM((CAND, rows), jnp.float32),
            pltpu.VMEM((M_ROWS, 2 * rows), jnp.bfloat16),
            pltpu.VMEM((2, BACK, feat), jnp.bfloat16),
            pltpu.VMEM((2, IN_ROWS, feat), jnp.bfloat16),
            pltpu.VMEM((2, 2, MESSAGE + HALF, feat), jnp.bfloat16),
            pltpu.VMEM((2, MESSAGE, feat), jnp.bfloat16),
            pltpu.SemaphoreType.DMA((4,)),
            pltpu.SemaphoreType.DMA((2, PIECES)),
            pltpu.SemaphoreType.DMA((2, PIECES)),
            pltpu.SemaphoreType.DMA((STAGES, CHUNKS)),
            pltpu.SemaphoreType.DMA((STAGES, CHUNKS)),
        ],
        compiler_params=pltpu.CompilerParams(
            collective_id=0, has_side_effects=True, vmem_limit_bytes=40 * 1024 * 1024),
    )(*(pltpu.with_memory_space_constraint(x, pltpu.HBM)
        for x in (queries, key_input, value_input, cotangent)))
    return tuple(pl.pallas_call(
        place,
        name="place",
        out_shape=[out] * 4,
        in_specs=[pl.BlockSpec(memory_space=pltpu.VMEM)] * 4,
        out_specs=[pl.BlockSpec(memory_space=pl.ANY)] * 4,
        scratch_shapes=[pltpu.SemaphoreType.DMA((4,))],
    )(*(pltpu.with_memory_space_constraint(x, pltpu.VMEM) for x in results)))


def solution(mesh):
    spec = P(("groups", "seq"), None)
    return jax.shard_map(
        body, mesh=mesh, in_specs=(spec,) * 4, out_specs=(spec,) * 4, check_vma=False)
```

```python
import math

import jax
import jax.numpy as jnp
from jax import lax
from jax.experimental import pallas as pl
from jax.experimental.pallas import tpu as pltpu
from jax.sharding import PartitionSpec as P

HEADS = 16
HEAD_DIM = 128
BLOCK = 64
HALF = BLOCK // 2
CHUNKS = 8
EARLY = 2
PIECES = 2
SHARE = 2
ATTEND = 3
OUTER = 4
PEER = 6
LAST = 9

SIB_FINE = 2 * BLOCK
OWN_COARSE = SIB_FINE + BLOCK
OWN_L2 = OWN_COARSE + BLOCK
COARSE = BLOCK + HALF
SIB_COARSE = OWN_COARSE + COARSE
OUT = SIB_COARSE + COARSE
FAR = OUT + 3 * BLOCK
CAND = FAR + BLOCK
RELAY = CAND
KV_ROWS = RELAY + 2 * BLOCK + HALF
MESSAGE = BLOCK + HALF
DERIVED = MESSAGE
SECOND = DERIVED + HALF
G_COARSE = 2 * BLOCK
G_OUT = G_COARSE + COARSE
GRAD_ROWS = G_OUT + 3 * BLOCK
B_FAR = BLOCK + COARSE
BACK = B_FAR + BLOCK
IN_ROWS = BACK + MESSAGE
M_MESSAGE = 0
M_OWN = M_MESSAGE + MESSAGE
M_SECOND = M_OWN + 2 * BLOCK
M_POOL = M_SECOND + MESSAGE
M_ROWS = M_POOL + HALF
STAGES = 9

masked_score = -1e30
MESH = pl.DeviceIdType.MESH


def nt(a, b):
    return lax.dot_general(a, b, (((1,), (1,)), ((), ())), preferred_element_type=jnp.float32)


def nn(a, b):
    return lax.dot_general(a, b, (((1,), (0,)), ((), ())), preferred_element_type=jnp.float32)


def tn(a, b):
    return lax.dot_general(a, b, (((0,), (0,)), ((), ())), preferred_element_type=jnp.float32)


def pool_matrix(rows):
    row = lax.broadcasted_iota(jnp.int32, (rows // 2, rows), 0)
    col = lax.broadcasted_iota(jnp.int32, (rows // 2, rows), 1)
    return jnp.where((col >> 1) == row, 0.5, 0.0).astype(jnp.bfloat16)


def pooled(rows):
    return nn(pool_matrix(rows.shape[0]), rows).astype(jnp.bfloat16)


def spread_matrix(shape, row0, col0, rows, shift):
    row = lax.broadcasted_iota(jnp.int32, shape, 0) - row0
    col = lax.broadcasted_iota(jnp.int32, shape, 1) - col0
    hit = (row >= 0) & (row < rows) & ((row >> shift) == col)
    return jnp.where(hit, 0.5 ** shift, 0.0)


def message_matrix():
    shape = (MESSAGE, BLOCK)
    return (spread_matrix(shape, 0, 0, BLOCK, 1)
            + spread_matrix(shape, 0, HALF, BLOCK, 2)
            + spread_matrix(shape, BLOCK, HALF + HALF // 2, HALF, 1)).astype(jnp.bfloat16)


def second_matrix():
    shape = (MESSAGE, HALF)
    return (spread_matrix(shape, 0, 0, BLOCK, 2)
            + spread_matrix(shape, BLOCK, HALF // 2, HALF, 1)).astype(jnp.bfloat16)


def own_matrix():
    shape = (2 * BLOCK, COARSE)
    return (spread_matrix(shape, 0, 0, 2 * BLOCK, 1)
            + spread_matrix(shape, 0, BLOCK, 2 * BLOCK, 2)).astype(jnp.bfloat16)


def split(rows):
    high = rows.astype(jnp.bfloat16)
    return high, (rows - high.astype(jnp.float32)).astype(jnp.bfloat16)


def kernel(queries, keys, values, cotangent, att_ref, gq_ref, gk_ref, gv_ref,
           q_ref, do_ref, kv, grad, bias, mats, back_out, arrived, pass_on, ret_out,
           load_sem, sib_send, sib_recv, send_sem, recv_sem):
    count = lax.axis_size("seq")
    me = lax.axis_index("seq")
    side = lax.rem(me, 2)
    chip = me // 2
    odd = lax.rem(chip, 2)
    sib = me + 1 - 2 * side
    p_role = lax.rem(side + chip, 2)
    d_role = 1 - p_role
    is_p = p_role == 1
    is_d = p_role == 0
    peer = 2 * (chip + 1 - 2 * odd) + 1 - side
    step = 4 - 8 * odd
    has_next = (me + step >= 0) & (me + step < count)
    has_prev = (me - step >= 0) & (me - step < count)
    has_outer = is_p | has_prev
    has_far = is_d | has_prev
    d_next = is_d & has_next
    d_prev = is_d & has_prev
    p_next = is_p & has_next
    feat = queries.shape[1]
    width = feat // CHUNKS
    heads = width // HEAD_DIM
    scale = HEAD_DIM ** -0.5
    inner_start = pl.multiple_of(BLOCK * (1 - side), BLOCK)
    outer_start = pl.multiple_of(BLOCK * side, BLOCK)
    inner_half = pl.multiple_of(HALF * (1 - side), HALF)
    landing = pl.multiple_of(OUT + (RELAY - OUT) * d_role, BLOCK)
    other = pl.multiple_of(OUT + (RELAY - OUT) * p_role, BLOCK)
    top = pl.multiple_of(BACK * (1 - side), HALF)
    bottom = pl.multiple_of(BACK * side, HALF)

    loads = [pltpu.make_async_copy(src, dst, load_sem.at[i]) for i, (src, dst) in enumerate((
        (keys, kv.at[0, 0:2 * BLOCK]), (values, kv.at[1, 0:2 * BLOCK]), (queries, q_ref), (cotangent, do_ref)))]
    for item in loads:
        item.start()

    barrier = pltpu.get_barrier_semaphore()

    def greet(target):
        pl.semaphore_signal(barrier, inc=1, device_id={"seq": target}, device_id_type=MESH)

    greet(sib)
    greet(peer)

    @pl.when(d_next)
    def _():
        greet(me + step)

    @pl.when(p_next)
    def _():
        greet(sib + step)

    @pl.when(d_prev)
    def _():
        greet(me - step)
        greet(sib - step)

    def pool_own(first, number):
        cols = pl.ds(first * width, number * width)
        for which in range(2):
            half = pooled(kv[which, 0:2 * BLOCK, cols])
            kv[which, OWN_COARSE:OWN_COARSE + BLOCK, cols] = half
            kv[which, OWN_L2:OWN_L2 + HALF, cols] = pooled(half)

    loads[0].wait()
    loads[1].wait()

    peers = 2 + has_next.astype(jnp.int32) + 2 * d_prev.astype(jnp.int32)
    pl.semaphore_wait(barrier, peers)

    def remote(src, dst, sends, recvs, target):
        return pltpu.make_async_remote_copy(
            src_ref=src, dst_ref=dst, send_sem=sends, recv_sem=recvs,
            device_id={"seq": target}, device_id_type=MESH)

    def copy(stage, g, src, src_row, dst, dst_row, rows, target):
        cols = pl.ds(g * width, width)
        return remote(src.at[:, pl.ds(src_row, rows), cols], dst.at[:, pl.ds(dst_row, rows), cols],
                      send_sem.at[stage, g], recv_sem.at[stage, g], target)

    def sib_copy(kind, piece):
        cols = pl.ds(piece * (feat // PIECES), feat // PIECES)
        src, dst, rows = ((inner_start, SIB_FINE, BLOCK), (OWN_COARSE, SIB_COARSE, COARSE))[kind]
        return remote(kv.at[:, pl.ds(src, rows), cols], kv.at[:, pl.ds(dst, rows), cols],
                      sib_send.at[kind, piece], sib_recv.at[kind, piece], sib)

    def y_fine(g):
        return copy(0, g, kv, outer_start, kv, landing, BLOCK, peer)

    def y_half(g):
        return copy(1, g, kv, OWN_COARSE + inner_half, kv, landing + BLOCK, HALF, peer)

    def z_rows(g):
        return copy(2, g, kv, RELAY, kv, OUT, MESSAGE, me + step)

    def second(g):
        return copy(3, g, kv, landing + SECOND, kv, OUT + SECOND + HALF, HALF, sib + step * p_role)

    def far(g):
        return copy(4, g, kv, OUT + SECOND, kv, FAR, BLOCK, sib)

    def back(g):
        return copy(5, g, back_out, 0, arrived, 0, BACK, sib)

    def z_grads(g):
        return copy(6, g, pass_on.at[0], 0, pass_on.at[1], 0, MESSAGE, me - step)

    def second_grads(g):
        return copy(7, g, pass_on.at[0], MESSAGE, pass_on.at[1], MESSAGE, HALF, sib - step * d_role)

    def ret(g):
        return copy(8, g, ret_out, 0, arrived, BACK, MESSAGE, peer)

    sends_second = is_d | p_next
    gets_second = is_p | d_prev

    for g in range(CHUNKS):
        if g == EARLY:
            pool_own(EARLY, CHUNKS - EARLY)
        if g == 0:
            for early in range(EARLY):
                y_fine(early).start()
            pool_own(0, EARLY)
        y_half(g).start()
        if EARLY <= g + 1 < CHUNKS:
            y_fine(g + 1).start()
    for piece in range(PIECES):
        sib_copy(0, piece).start()
        sib_copy(1, piece).start()

    @pl.when(jnp.logical_not(has_outer))
    def _():
        kv[:, OUT:OUT + 3 * BLOCK, :] = jnp.zeros((2, 3 * BLOCK, feat), jnp.bfloat16)

    @pl.when(is_d & jnp.logical_not(has_next))
    def _():
        pass_on[1, :, 0:MESSAGE, :] = jnp.zeros((2, MESSAGE, feat), jnp.bfloat16)

    @pl.when(is_p & jnp.logical_not(has_next))
    def _():
        pass_on[1, :, MESSAGE:MESSAGE + HALF, :] = jnp.zeros((2, HALF, feat), jnp.bfloat16)

    lane = lax.broadcasted_iota(jnp.int32, (BLOCK, 2 * BLOCK), 1)
    is_outer_lane = (lane >> 6) == side
    zero = jnp.zeros((BLOCK, 2 * BLOCK), jnp.float32)
    for row in (0, BLOCK):
        bias[row:row + BLOCK] = zero
    bias[SIB_FINE:SIB_FINE + BLOCK] = jnp.where(is_outer_lane, masked_score, zero)
    for row in (OWN_COARSE, SIB_COARSE):
        bias[row:row + BLOCK] = zero + 1.0
        bias[row + BLOCK:row + COARSE] = zero[:HALF] + 2.0
    bias[OUT:OUT + BLOCK] = jnp.where(is_outer_lane & has_outer, zero, masked_score)
    bias[OUT + BLOCK:OUT + 2 * BLOCK] = jnp.where(has_outer, zero + 1.0, masked_score)
    bias[OUT + SECOND:OUT + 3 * BLOCK] = jnp.where(has_outer, zero + 2.0, masked_score)
    bias[FAR:FAR + BLOCK] = jnp.where(has_far, zero + 2.0, masked_score)

    message = message_matrix()
    mats[M_MESSAGE:M_MESSAGE + MESSAGE, 0:2 * BLOCK] = jnp.concatenate([message, message], axis=1)
    own = own_matrix()
    inner = spread_matrix((2 * BLOCK, HALF), inner_start, 0, BLOCK, 1).astype(jnp.bfloat16)
    mats[M_OWN:M_OWN + 2 * BLOCK, 0:2 * COARSE + HALF] = jnp.concatenate([own, inner, own], axis=1)
    mats[M_SECOND:M_SECOND + MESSAGE, 0:HALF] = second_matrix()
    mats[M_POOL:M_POOL + HALF, 0:BLOCK] = pool_matrix(BLOCK)

    def columns(g):
        return pl.ds(g * width, width)

    def derive(base, g):
        cols = columns(g)
        pool = mats[M_POOL:M_POOL + HALF, 0:BLOCK]
        for which in range(2):
            first = nn(pool, kv[which, pl.ds(base, BLOCK), cols]).astype(jnp.bfloat16)
            both = jnp.concatenate([first, kv[which, pl.ds(base + BLOCK, HALF), cols]], axis=0)
            kv[which, pl.ds(base + DERIVED, HALF), cols] = first
            kv[which, pl.ds(base + SECOND, HALF), cols] = nn(pool, both).astype(jnp.bfloat16)

    def store_parts(which, part, cols):
        for dst, src, rows in ((0, 0, 2 * BLOCK), (G_COARSE, OWN_COARSE, COARSE), (G_OUT, OUT, 3 * BLOCK)):
            grad[which, dst:dst + rows, cols] = part[src:src + rows]
        for dst, src, rows in ((0, SIB_FINE, BLOCK), (BLOCK, SIB_COARSE, COARSE), (B_FAR, FAR, BLOCK)):
            back_out[which, dst:dst + rows, cols] = part[src:src + rows].astype(jnp.bfloat16)

    def attend(first, number):
        def score(h):
            cols = pl.ds(h * HEAD_DIM, HEAD_DIM)
            scores = nt(kv[0, 0:CAND, cols], q_ref[:, cols]) * (scale * math.log2(math.e)) + bias[...]
            grad_weights = nt(kv[1, 0:CAND, cols], do_ref[:, cols])
            return scores, grad_weights, jnp.max(scores, axis=0, keepdims=True)

        def weigh(scores, grad_weights, largest):
            raised = jnp.exp2(scores - largest)
            weights = raised * (1.0 / jnp.sum(raised, axis=0, keepdims=True))
            row_dots = jnp.sum(weights * grad_weights, axis=0, keepdims=True)
            grad_scores = weights * ((grad_weights - row_dots) * scale)
            return weights.astype(jnp.bfloat16), grad_scores.astype(jnp.bfloat16)

        def combine(h, weights_b, grad_scores):
            cols = pl.ds(h * HEAD_DIM, HEAD_DIM)
            att_ref[:, cols] = tn(weights_b, kv[1, 0:CAND, cols]).astype(jnp.bfloat16)
            store_parts(1, nn(weights_b, do_ref[:, cols]), cols)
            gq_ref[:, cols] = tn(grad_scores, kv[0, 0:CAND, cols]).astype(jnp.bfloat16)
            store_parts(0, nn(grad_scores, q_ref[:, cols]), cols)

        fronts = [score(first + i) for i in range(number)]
        for i, front in enumerate(fronts):
            combine(first + i, *weigh(*front))

    def fold(g):
        cols = columns(g)
        matrix = mats[M_MESSAGE:M_MESSAGE + MESSAGE, 0:2 * BLOCK]
        for which in range(2):
            second = (grad[which, G_OUT + SECOND:GRAD_ROWS, cols]
                      + arrived[which, B_FAR:BACK, cols].astype(jnp.float32))
            coarse = jnp.concatenate([grad[which, G_OUT + DERIVED:G_OUT + SECOND, cols], second[:HALF]], axis=0)
            total = nn(matrix, jnp.concatenate(split(coarse), axis=0)) + grad[which, G_OUT:G_OUT + MESSAGE, cols]
            pass_on[0, which, 0:MESSAGE, cols] = total.astype(jnp.bfloat16)
            pass_on[0, which, MESSAGE:MESSAGE + HALF, cols] = second[HALF:].astype(jnp.bfloat16)

    def gather(g):
        cols = columns(g)
        matrix = mats[M_SECOND:M_SECOND + MESSAGE, 0:HALF]
        for which in range(2):
            total = nn(matrix, pass_on[1, which, MESSAGE:MESSAGE + HALF, cols])
            total += pass_on[d_role, which, 0:MESSAGE, cols].astype(jnp.float32)
            ret_out[which, :, cols] = total.astype(jnp.bfloat16)

    def finish(g):
        cols = columns(g)
        matrix = mats[M_OWN:M_OWN + 2 * BLOCK, 0:2 * COARSE + HALF]
        for which, ref in enumerate((gk_ref, gv_ref)):
            coarse = (grad[which, G_COARSE:G_OUT, cols]
                      + arrived[which, BLOCK:BLOCK + COARSE, cols].astype(jnp.float32))
            high, low = split(coarse)
            parts = jnp.concatenate([high, arrived[which, BACK + BLOCK:IN_ROWS, cols], low], axis=0)
            fine = jnp.concatenate([arrived[which, pl.ds(top, BLOCK), cols],
                                    arrived[which, pl.ds(bottom, BLOCK), cols]], axis=0)
            total = nn(matrix, parts) + (grad[which, 0:2 * BLOCK, cols] + fine.astype(jnp.float32))
            ref[:, cols] = total.astype(jnp.bfloat16)

    def when(cond, item, act):
        @pl.when(cond)
        def _():
            getattr(item, act)()

    loads[2].wait()
    loads[3].wait()
    for i in range(CHUNKS + LAST):
        def now(lag):
            return 0 <= i - lag < CHUNKS

        if now(0):
            y_fine(i).wait_recv()
            y_half(i).wait_recv()
            when(d_next, z_rows(i), "start")
        if now(SHARE):
            when(d_prev, z_rows(i - SHARE), "wait_recv")
            when(gets_second, second(i - SHARE), "wait_recv")
        if now(0):
            derive(landing, i)
        if now(SHARE):
            derive(other, i - SHARE)
            far(i - SHARE).start()
        if now(0):
            when(sends_second, second(i), "start")
        if now(ATTEND):
            g = i - ATTEND
            if g % (CHUNKS // PIECES) == 0:
                for kind in range(2):
                    sib_copy(kind, g // (CHUNKS // PIECES)).wait_recv()
            far(g).wait_recv()
            attend(g * heads, heads)
            back(g).start()
        if now(OUTER):
            back(i - OUTER).wait_recv()
            fold(i - OUTER)
            when(d_prev, z_grads(i - OUTER), "start")
            when(gets_second, second_grads(i - OUTER), "start")
        if now(PEER):
            when(d_next, z_grads(i - PEER), "wait_recv")
            when(sends_second, second_grads(i - PEER), "wait_recv")
            gather(i - PEER)
            ret(i - PEER).start()
        if now(LAST):
            ret(i - LAST).wait_recv()
            finish(i - LAST)

    for piece in range(PIECES):
        for kind in range(2):
            sib_copy(kind, piece).wait_send()
    for g in range(CHUNKS):
        for item in (y_fine, y_half, far, back, ret):
            item(g).wait_send()
        when(sends_second, second(g), "wait_send")
        when(d_next, z_rows(g), "wait_send")
        when(d_prev, z_grads(g), "wait_send")
        when(gets_second, second_grads(g), "wait_send")


def place(*refs):
    sems = refs[8]
    stores = [pltpu.make_async_copy(refs[i], refs[4 + i], sems.at[i]) for i in range(4)]
    for item in stores:
        item.start()
    for item in stores:
        item.wait()


def body(queries, key_input, value_input, cotangent):
    rows, feat = queries.shape
    out = jax.ShapeDtypeStruct((rows, feat), jnp.bfloat16)
    results = pl.pallas_call(
        kernel,
        name="hier_attention",
        out_shape=[pltpu.VMEM((rows, feat), jnp.bfloat16)] * 4,
        in_specs=[pl.BlockSpec(memory_space=pl.ANY)] * 4,
        out_specs=[pl.BlockSpec(memory_space=pltpu.VMEM)] * 4,
        scratch_shapes=[
            pltpu.VMEM((rows, feat), jnp.bfloat16),
            pltpu.VMEM((rows, feat), jnp.bfloat16),
            pltpu.VMEM((2, KV_ROWS, feat), jnp.bfloat16),
            pltpu.VMEM((2, GRAD_ROWS, feat), jnp.float32),
            pltpu.VMEM((CAND, rows), jnp.float32),
            pltpu.VMEM((M_ROWS, 2 * rows), jnp.bfloat16),
            pltpu.VMEM((2, BACK, feat), jnp.bfloat16),
            pltpu.VMEM((2, IN_ROWS, feat), jnp.bfloat16),
            pltpu.VMEM((2, 2, MESSAGE + HALF, feat), jnp.bfloat16),
            pltpu.VMEM((2, MESSAGE, feat), jnp.bfloat16),
            pltpu.SemaphoreType.DMA((4,)),
            pltpu.SemaphoreType.DMA((2, PIECES)),
            pltpu.SemaphoreType.DMA((2, PIECES)),
            pltpu.SemaphoreType.DMA((STAGES, CHUNKS)),
            pltpu.SemaphoreType.DMA((STAGES, CHUNKS)),
        ],
        compiler_params=pltpu.CompilerParams(
            collective_id=0, has_side_effects=True, vmem_limit_bytes=40 * 1024 * 1024),
    )(*(pltpu.with_memory_space_constraint(x, pltpu.HBM)
        for x in (queries, key_input, value_input, cotangent)))
    return tuple(pl.pallas_call(
        place,
        name="place",
        out_shape=[out] * 4,
        in_specs=[pl.BlockSpec(memory_space=pltpu.VMEM)] * 4,
        out_specs=[pl.BlockSpec(memory_space=pl.ANY)] * 4,
        scratch_shapes=[pltpu.SemaphoreType.DMA((4,))],
    )(*(pltpu.with_memory_space_constraint(x, pltpu.VMEM) for x in results)))


def solution(mesh):
    spec = P(("groups", "seq"), None)
    return jax.shard_map(
        body, mesh=mesh, in_specs=(spec,) * 4, out_specs=(spec,) * 4, check_vma=False)
```

```python
import math

import jax
import jax.numpy as jnp
from jax import lax
from jax.experimental import pallas as pl
from jax.experimental.pallas import tpu as pltpu
from jax.sharding import PartitionSpec as P

HEADS = 16
HEAD_DIM = 128
BLOCK = 64
HALF = BLOCK // 2
PARTS = (2, 2, 2, 2, 2, 2, 2, 2)
STARTS = tuple(sum(PARTS[:g]) for g in range(len(PARTS)))
CHUNKS = len(PARTS)
EARLY = 2
PIECES = 2
LAGS = dict(take=0, attend=2, outer=3, gather=5, share=1, finish=9)

SIB_FINE = 2 * BLOCK
OWN_COARSE = SIB_FINE + BLOCK
OWN_L2 = OWN_COARSE + BLOCK
COARSE = BLOCK + HALF
SIB_COARSE = OWN_COARSE + COARSE
OUT = SIB_COARSE + COARSE
FAR = OUT + 3 * BLOCK
CAND = FAR + BLOCK
RELAY = CAND
KV_ROWS = RELAY + 2 * BLOCK + HALF
MESSAGE = BLOCK + HALF
DERIVED = MESSAGE
SECOND = DERIVED + HALF
G_COARSE = 2 * BLOCK
G_OUT = G_COARSE + COARSE
GRAD_ROWS = G_OUT + 3 * BLOCK
B_FAR = BLOCK + COARSE
BACK = B_FAR + BLOCK
IN_ROWS = BACK + MESSAGE
M_MESSAGE = 0
M_OWN = M_MESSAGE + MESSAGE
M_SECOND = M_OWN + 2 * BLOCK
M_POOL = M_SECOND + MESSAGE
M_ROWS = M_POOL + HALF
STAGES = 9

masked_score = -1e30
MESH = pl.DeviceIdType.MESH


def plan():
    return [(stage, i - LAGS[stage]) for i in range(CHUNKS + max(LAGS.values()))
            for stage in LAGS if 0 <= i - LAGS[stage] < CHUNKS]


def nt(a, b):
    return lax.dot_general(a, b, (((1,), (1,)), ((), ())), preferred_element_type=jnp.float32)


def nn(a, b):
    return lax.dot_general(a, b, (((1,), (0,)), ((), ())), preferred_element_type=jnp.float32)


def tn(a, b):
    return lax.dot_general(a, b, (((0,), (0,)), ((), ())), preferred_element_type=jnp.float32)


def pool_matrix(rows):
    row = lax.broadcasted_iota(jnp.int32, (rows // 2, rows), 0)
    col = lax.broadcasted_iota(jnp.int32, (rows // 2, rows), 1)
    return jnp.where((col >> 1) == row, 0.5, 0.0).astype(jnp.bfloat16)


def pooled(rows):
    return nn(pool_matrix(rows.shape[0]), rows).astype(jnp.bfloat16)


def spread_matrix(shape, row0, col0, rows, shift):
    row = lax.broadcasted_iota(jnp.int32, shape, 0) - row0
    col = lax.broadcasted_iota(jnp.int32, shape, 1) - col0
    hit = (row >= 0) & (row < rows) & ((row >> shift) == col)
    return jnp.where(hit, 0.5 ** shift, 0.0)


def message_matrix():
    shape = (MESSAGE, BLOCK)
    return (spread_matrix(shape, 0, 0, BLOCK, 1)
            + spread_matrix(shape, 0, HALF, BLOCK, 2)
            + spread_matrix(shape, BLOCK, HALF + HALF // 2, HALF, 1)).astype(jnp.bfloat16)


def second_matrix():
    shape = (MESSAGE, HALF)
    return (spread_matrix(shape, 0, 0, BLOCK, 2)
            + spread_matrix(shape, BLOCK, HALF // 2, HALF, 1)).astype(jnp.bfloat16)


def own_matrix():
    shape = (2 * BLOCK, COARSE)
    return (spread_matrix(shape, 0, 0, 2 * BLOCK, 1)
            + spread_matrix(shape, 0, BLOCK, 2 * BLOCK, 2)).astype(jnp.bfloat16)


def split(rows):
    high = rows.astype(jnp.bfloat16)
    return high, (rows - high.astype(jnp.float32)).astype(jnp.bfloat16)


def kernel(queries, keys, values, cotangent, att_ref, gq_ref, gk_ref, gv_ref,
           q_ref, do_ref, kv, grad, bias, mats, back_out, arrived, pass_on, ret_out,
           load_sem, sib_send, sib_recv, send_sem, recv_sem):
    count = lax.axis_size("seq")
    me = lax.axis_index("seq")
    side = lax.rem(me, 2)
    chip = me // 2
    odd = lax.rem(chip, 2)
    sib = me + 1 - 2 * side
    p_role = lax.rem(side + chip, 2)
    d_role = 1 - p_role
    is_p = p_role == 1
    is_d = p_role == 0
    peer = 2 * (chip + 1 - 2 * odd) + 1 - side
    step = 4 - 8 * odd
    has_next = (me + step >= 0) & (me + step < count)
    has_prev = (me - step >= 0) & (me - step < count)
    has_outer = is_p | has_prev
    has_far = is_d | has_prev
    d_next = is_d & has_next
    d_prev = is_d & has_prev
    p_next = is_p & has_next
    feat = queries.shape[1]
    scale = HEAD_DIM ** -0.5
    inner_start = pl.multiple_of(BLOCK * (1 - side), BLOCK)
    outer_start = pl.multiple_of(BLOCK * side, BLOCK)
    inner_half = pl.multiple_of(HALF * (1 - side), HALF)
    landing = pl.multiple_of(OUT + (RELAY - OUT) * d_role, BLOCK)
    other = pl.multiple_of(OUT + (RELAY - OUT) * p_role, BLOCK)
    top = pl.multiple_of(BACK * (1 - side), HALF)
    bottom = pl.multiple_of(BACK * side, HALF)

    loads = [pltpu.make_async_copy(src, dst, load_sem.at[i]) for i, (src, dst) in enumerate((
        (keys, kv.at[0, 0:2 * BLOCK]), (values, kv.at[1, 0:2 * BLOCK]), (queries, q_ref), (cotangent, do_ref)))]
    for item in loads:
        item.start()

    barrier = pltpu.get_barrier_semaphore()

    def greet(target):
        pl.semaphore_signal(barrier, inc=1, device_id={"seq": target}, device_id_type=MESH)

    greet(sib)
    greet(peer)

    @pl.when(d_next)
    def _():
        greet(me + step)

    @pl.when(p_next)
    def _():
        greet(sib + step)

    @pl.when(d_prev)
    def _():
        greet(me - step)
        greet(sib - step)

    def columns(g):
        return pl.ds(STARTS[g] * HEAD_DIM, PARTS[g] * HEAD_DIM)

    def pool_own(first, number):
        cols = pl.ds(STARTS[first] * HEAD_DIM, sum(PARTS[first:first + number]) * HEAD_DIM)
        for which in range(2):
            half = pooled(kv[which, 0:2 * BLOCK, cols])
            kv[which, OWN_COARSE:OWN_COARSE + BLOCK, cols] = half
            kv[which, OWN_L2:OWN_L2 + HALF, cols] = pooled(half)

    loads[0].wait()
    loads[1].wait()

    peers = 2 + has_next.astype(jnp.int32) + 2 * d_prev.astype(jnp.int32)
    pl.semaphore_wait(barrier, peers)

    def remote(src, dst, sends, recvs, target):
        return pltpu.make_async_remote_copy(
            src_ref=src, dst_ref=dst, send_sem=sends, recv_sem=recvs,
            device_id={"seq": target}, device_id_type=MESH)

    def copy(stage, g, src, src_row, dst, dst_row, rows, target):
        cols = columns(g)
        return remote(src.at[:, pl.ds(src_row, rows), cols], dst.at[:, pl.ds(dst_row, rows), cols],
                      send_sem.at[stage, g], recv_sem.at[stage, g], target)

    def sib_copy(kind, piece):
        cols = pl.ds(piece * (feat // PIECES), feat // PIECES)
        src, dst, rows = ((inner_start, SIB_FINE, BLOCK), (OWN_COARSE, SIB_COARSE, COARSE))[kind]
        return remote(kv.at[:, pl.ds(src, rows), cols], kv.at[:, pl.ds(dst, rows), cols],
                      sib_send.at[kind, piece], sib_recv.at[kind, piece], sib)

    def y_fine(g):
        return copy(0, g, kv, outer_start, kv, landing, BLOCK, peer)

    def y_half(g):
        return copy(1, g, kv, OWN_COARSE + inner_half, kv, landing + BLOCK, HALF, peer)

    def z_rows(g):
        return copy(2, g, kv, RELAY, kv, OUT, MESSAGE, me + step)

    def second(g):
        return copy(3, g, kv, landing + SECOND, kv, OUT + SECOND + HALF, HALF, sib + step * p_role)

    def far(g):
        return copy(4, g, kv, OUT + SECOND, kv, FAR, BLOCK, sib)

    def back(g):
        return copy(5, g, back_out, 0, arrived, 0, BACK, sib)

    def z_grads(g):
        return copy(6, g, pass_on.at[0], 0, pass_on.at[1], 0, MESSAGE, me - step)

    def second_grads(g):
        return copy(7, g, pass_on.at[0], MESSAGE, pass_on.at[1], MESSAGE, HALF, sib - step * d_role)

    def ret(g):
        return copy(8, g, ret_out, 0, arrived, BACK, MESSAGE, peer)

    sends_second = is_d | p_next
    gets_second = is_p | d_prev

    for g in range(CHUNKS):
        if g == EARLY:
            pool_own(EARLY, CHUNKS - EARLY)
        if g == 0:
            for early in range(EARLY):
                y_fine(early).start()
            pool_own(0, EARLY)
        y_half(g).start()
        if EARLY <= g + 1 < CHUNKS:
            y_fine(g + 1).start()
    for piece in range(PIECES):
        sib_copy(0, piece).start()
        sib_copy(1, piece).start()

    @pl.when(jnp.logical_not(has_outer))
    def _():
        kv[:, OUT:OUT + 3 * BLOCK, :] = jnp.zeros((2, 3 * BLOCK, feat), jnp.bfloat16)

    @pl.when(is_d & jnp.logical_not(has_next))
    def _():
        pass_on[1, :, 0:MESSAGE, :] = jnp.zeros((2, MESSAGE, feat), jnp.bfloat16)

    @pl.when(is_p & jnp.logical_not(has_next))
    def _():
        pass_on[1, :, MESSAGE:MESSAGE + HALF, :] = jnp.zeros((2, HALF, feat), jnp.bfloat16)

    lane = lax.broadcasted_iota(jnp.int32, (BLOCK, 2 * BLOCK), 1)
    is_outer_lane = (lane >> 6) == side
    zero = jnp.zeros((BLOCK, 2 * BLOCK), jnp.float32)
    for row in (0, BLOCK):
        bias[row:row + BLOCK] = zero
    bias[SIB_FINE:SIB_FINE + BLOCK] = jnp.where(is_outer_lane, masked_score, zero)
    for row in (OWN_COARSE, SIB_COARSE):
        bias[row:row + BLOCK] = zero + 1.0
        bias[row + BLOCK:row + COARSE] = zero[:HALF] + 2.0
    bias[OUT:OUT + BLOCK] = jnp.where(is_outer_lane & has_outer, zero, masked_score)
    bias[OUT + BLOCK:OUT + 2 * BLOCK] = jnp.where(has_outer, zero + 1.0, masked_score)
    bias[OUT + SECOND:OUT + 3 * BLOCK] = jnp.where(has_outer, zero + 2.0, masked_score)
    bias[FAR:FAR + BLOCK] = jnp.where(has_far, zero + 2.0, masked_score)

    message = message_matrix()
    mats[M_MESSAGE:M_MESSAGE + MESSAGE, 0:2 * BLOCK] = jnp.concatenate([message, message], axis=1)
    own = own_matrix()
    inner = spread_matrix((2 * BLOCK, HALF), inner_start, 0, BLOCK, 1).astype(jnp.bfloat16)
    mats[M_OWN:M_OWN + 2 * BLOCK, 0:2 * COARSE + HALF] = jnp.concatenate([own, inner, own], axis=1)
    mats[M_SECOND:M_SECOND + MESSAGE, 0:HALF] = second_matrix()
    mats[M_POOL:M_POOL + HALF, 0:BLOCK] = pool_matrix(BLOCK)

    def derive(base, g):
        cols = columns(g)
        pool = mats[M_POOL:M_POOL + HALF, 0:BLOCK]
        for which in range(2):
            first = nn(pool, kv[which, pl.ds(base, BLOCK), cols]).astype(jnp.bfloat16)
            both = jnp.concatenate([first, kv[which, pl.ds(base + BLOCK, HALF), cols]], axis=0)
            kv[which, pl.ds(base + DERIVED, HALF), cols] = first
            kv[which, pl.ds(base + SECOND, HALF), cols] = nn(pool, both).astype(jnp.bfloat16)

    def store_parts(which, part, cols):
        for dst, src, rows in ((0, 0, 2 * BLOCK), (G_COARSE, OWN_COARSE, COARSE), (G_OUT, OUT, 3 * BLOCK)):
            grad[which, dst:dst + rows, cols] = part[src:src + rows]
        for dst, src, rows in ((0, SIB_FINE, BLOCK), (BLOCK, SIB_COARSE, COARSE), (B_FAR, FAR, BLOCK)):
            back_out[which, dst:dst + rows, cols] = part[src:src + rows].astype(jnp.bfloat16)

    def attend(first, number):
        def score(h):
            cols = pl.ds(h * HEAD_DIM, HEAD_DIM)
            scores = nt(kv[0, 0:CAND, cols], q_ref[:, cols]) * (scale * math.log2(math.e)) + bias[...]
            grad_weights = nt(kv[1, 0:CAND, cols], do_ref[:, cols])
            return scores, grad_weights, jnp.max(scores, axis=0, keepdims=True)

        def weigh(scores, grad_weights, largest):
            raised = jnp.exp2(scores - largest)
            weights = raised * (1.0 / jnp.sum(raised, axis=0, keepdims=True))
            row_dots = jnp.sum(weights * grad_weights, axis=0, keepdims=True)
            grad_scores = weights * ((grad_weights - row_dots) * scale)
            return weights.astype(jnp.bfloat16), grad_scores.astype(jnp.bfloat16)

        def combine(h, weights_b, grad_scores):
            cols = pl.ds(h * HEAD_DIM, HEAD_DIM)
            att_ref[:, cols] = tn(weights_b, kv[1, 0:CAND, cols]).astype(jnp.bfloat16)
            store_parts(1, nn(weights_b, do_ref[:, cols]), cols)
            gq_ref[:, cols] = tn(grad_scores, kv[0, 0:CAND, cols]).astype(jnp.bfloat16)
            store_parts(0, nn(grad_scores, q_ref[:, cols]), cols)

        fronts = [score(first + i) for i in range(number)]
        for i, front in enumerate(fronts):
            combine(first + i, *weigh(*front))

    def fold(g):
        cols = columns(g)
        matrix = mats[M_MESSAGE:M_MESSAGE + MESSAGE, 0:2 * BLOCK]
        for which in range(2):
            second = (grad[which, G_OUT + SECOND:GRAD_ROWS, cols]
                      + arrived[which, B_FAR:BACK, cols].astype(jnp.float32))
            coarse = jnp.concatenate([grad[which, G_OUT + DERIVED:G_OUT + SECOND, cols], second[:HALF]], axis=0)
            total = nn(matrix, jnp.concatenate(split(coarse), axis=0)) + grad[which, G_OUT:G_OUT + MESSAGE, cols]
            pass_on[0, which, 0:MESSAGE, cols] = total.astype(jnp.bfloat16)
            pass_on[0, which, MESSAGE:MESSAGE + HALF, cols] = second[HALF:].astype(jnp.bfloat16)

    def gather(g):
        cols = columns(g)
        matrix = mats[M_SECOND:M_SECOND + MESSAGE, 0:HALF]
        for which in range(2):
            total = nn(matrix, pass_on[1, which, MESSAGE:MESSAGE + HALF, cols])
            total += pass_on[d_role, which, 0:MESSAGE, cols].astype(jnp.float32)
            ret_out[which, :, cols] = total.astype(jnp.bfloat16)

    def finish(g):
        cols = columns(g)
        matrix = mats[M_OWN:M_OWN + 2 * BLOCK, 0:2 * COARSE + HALF]
        for which, ref in enumerate((gk_ref, gv_ref)):
            coarse = (grad[which, G_COARSE:G_OUT, cols]
                      + arrived[which, BLOCK:BLOCK + COARSE, cols].astype(jnp.float32))
            high, low = split(coarse)
            parts = jnp.concatenate([high, arrived[which, BACK + BLOCK:IN_ROWS, cols], low], axis=0)
            fine = jnp.concatenate([arrived[which, pl.ds(top, BLOCK), cols],
                                    arrived[which, pl.ds(bottom, BLOCK), cols]], axis=0)
            total = nn(matrix, parts) + (grad[which, 0:2 * BLOCK, cols] + fine.astype(jnp.float32))
            ref[:, cols] = total.astype(jnp.bfloat16)

    def when(cond, item, act):
        @pl.when(cond)
        def _():
            getattr(item, act)()

    loads[2].wait()
    loads[3].wait()
    have = 0
    for stage, g in plan():
        if stage == "take":
            y_fine(g).wait_recv()
            y_half(g).wait_recv()
            when(d_next, z_rows(g), "start")
            derive(landing, g)
            when(sends_second, second(g), "start")
        elif stage == "share":
            when(d_prev, z_rows(g), "wait_recv")
            when(gets_second, second(g), "wait_recv")
            derive(other, g)
            far(g).start()
        elif stage == "attend":
            while have * HEADS < (STARTS[g] + PARTS[g]) * PIECES:
                for kind in range(2):
                    sib_copy(kind, have).wait_recv()
                have += 1
            far(g).wait_recv()
            attend(STARTS[g], PARTS[g])
            back(g).start()
        elif stage == "outer":
            back(g).wait_recv()
            fold(g)
            when(d_prev, z_grads(g), "start")
            when(gets_second, second_grads(g), "start")
        elif stage == "gather":
            when(d_next, z_grads(g), "wait_recv")
            when(sends_second, second_grads(g), "wait_recv")
            gather(g)
            ret(g).start()
        else:
            ret(g).wait_recv()
            finish(g)

    for piece in range(PIECES):
        for kind in range(2):
            sib_copy(kind, piece).wait_send()
    for g in range(CHUNKS):
        for item in (y_fine, y_half, far, back, ret):
            item(g).wait_send()
        when(sends_second, second(g), "wait_send")
        when(d_next, z_rows(g), "wait_send")
        when(d_prev, z_grads(g), "wait_send")
        when(gets_second, second_grads(g), "wait_send")


def place(*refs):
    sems = refs[8]
    stores = [pltpu.make_async_copy(refs[i], refs[4 + i], sems.at[i]) for i in range(4)]
    for item in stores:
        item.start()
    for item in stores:
        item.wait()


def body(queries, key_input, value_input, cotangent):
    rows, feat = queries.shape
    out = jax.ShapeDtypeStruct((rows, feat), jnp.bfloat16)
    results = pl.pallas_call(
        kernel,
        name="hier_attention",
        out_shape=[pltpu.VMEM((rows, feat), jnp.bfloat16)] * 4,
        in_specs=[pl.BlockSpec(memory_space=pl.ANY)] * 4,
        out_specs=[pl.BlockSpec(memory_space=pltpu.VMEM)] * 4,
        scratch_shapes=[
            pltpu.VMEM((rows, feat), jnp.bfloat16),
            pltpu.VMEM((rows, feat), jnp.bfloat16),
            pltpu.VMEM((2, KV_ROWS, feat), jnp.bfloat16),
            pltpu.VMEM((2, GRAD_ROWS, feat), jnp.float32),
            pltpu.VMEM((CAND, rows), jnp.float32),
            pltpu.VMEM((M_ROWS, 2 * rows), jnp.bfloat16),
            pltpu.VMEM((2, BACK, feat), jnp.bfloat16),
            pltpu.VMEM((2, IN_ROWS, feat), jnp.bfloat16),
            pltpu.VMEM((2, 2, MESSAGE + HALF, feat), jnp.bfloat16),
            pltpu.VMEM((2, MESSAGE, feat), jnp.bfloat16),
            pltpu.SemaphoreType.DMA((4,)),
            pltpu.SemaphoreType.DMA((2, PIECES)),
            pltpu.SemaphoreType.DMA((2, PIECES)),
            pltpu.SemaphoreType.DMA((STAGES, CHUNKS)),
            pltpu.SemaphoreType.DMA((STAGES, CHUNKS)),
        ],
        compiler_params=pltpu.CompilerParams(
            collective_id=0, has_side_effects=True, vmem_limit_bytes=40 * 1024 * 1024),
    )(*(pltpu.with_memory_space_constraint(x, pltpu.HBM)
        for x in (queries, key_input, value_input, cotangent)))
    return tuple(pl.pallas_call(
        place,
        name="place",
        out_shape=[out] * 4,
        in_specs=[pl.BlockSpec(memory_space=pltpu.VMEM)] * 4,
        out_specs=[pl.BlockSpec(memory_space=pl.ANY)] * 4,
        scratch_shapes=[pltpu.SemaphoreType.DMA((4,))],
    )(*(pltpu.with_memory_space_constraint(x, pltpu.VMEM) for x in results)))


def solution(mesh):
    spec = P(("groups", "seq"), None)
    return jax.shard_map(
        body, mesh=mesh, in_specs=(spec,) * 4, out_specs=(spec,) * 4, check_vma=False)
```

```python
import math

import jax
import jax.numpy as jnp
from jax import lax
from jax.experimental import pallas as pl
from jax.experimental.pallas import tpu as pltpu
from jax.sharding import PartitionSpec as P

HEADS = 16
HEAD_DIM = 128
BLOCK = 64
HALF = BLOCK // 2
CHUNKS = 8
EARLY = 2
PIECES = 2
SHARE = 2
ATTEND = 3
OUTER = 4
PEER = 6
AHEAD = 1
LAST = 9

SIB_FINE = 2 * BLOCK
OWN_COARSE = SIB_FINE + BLOCK
OWN_L2 = OWN_COARSE + BLOCK
COARSE = BLOCK + HALF
SIB_COARSE = OWN_COARSE + COARSE
OUT = SIB_COARSE + COARSE
FAR = OUT + 3 * BLOCK
CAND = FAR + BLOCK
RELAY = CAND
KV_ROWS = RELAY + 2 * BLOCK + HALF
MESSAGE = BLOCK + HALF
DERIVED = MESSAGE
SECOND = DERIVED + HALF
G_COARSE = 2 * BLOCK
G_OUT = G_COARSE + COARSE
GRAD_ROWS = G_OUT + 3 * BLOCK
B_FAR = BLOCK + COARSE
BACK = B_FAR + BLOCK
IN_ROWS = BACK + MESSAGE
M_MESSAGE = 0
M_OWN = M_MESSAGE + MESSAGE
M_SECOND = M_OWN + 2 * BLOCK
M_POOL = M_SECOND + MESSAGE
M_ROWS = M_POOL + HALF
STAGES = 9

masked_score = -1e30
MESH = pl.DeviceIdType.MESH


def nt(a, b):
    return lax.dot_general(a, b, (((1,), (1,)), ((), ())), preferred_element_type=jnp.float32)


def nn(a, b):
    return lax.dot_general(a, b, (((1,), (0,)), ((), ())), preferred_element_type=jnp.float32)


def tn(a, b):
    return lax.dot_general(a, b, (((0,), (0,)), ((), ())), preferred_element_type=jnp.float32)


def pool_matrix(rows):
    row = lax.broadcasted_iota(jnp.int32, (rows // 2, rows), 0)
    col = lax.broadcasted_iota(jnp.int32, (rows // 2, rows), 1)
    return jnp.where((col >> 1) == row, 0.5, 0.0).astype(jnp.bfloat16)


def pooled(rows):
    return nn(pool_matrix(rows.shape[0]), rows).astype(jnp.bfloat16)


def spread_matrix(shape, row0, col0, rows, shift):
    row = lax.broadcasted_iota(jnp.int32, shape, 0) - row0
    col = lax.broadcasted_iota(jnp.int32, shape, 1) - col0
    hit = (row >= 0) & (row < rows) & ((row >> shift) == col)
    return jnp.where(hit, 0.5 ** shift, 0.0)


def message_matrix():
    shape = (MESSAGE, BLOCK)
    return (spread_matrix(shape, 0, 0, BLOCK, 1)
            + spread_matrix(shape, 0, HALF, BLOCK, 2)
            + spread_matrix(shape, BLOCK, HALF + HALF // 2, HALF, 1)).astype(jnp.bfloat16)


def second_matrix():
    shape = (MESSAGE, HALF)
    return (spread_matrix(shape, 0, 0, BLOCK, 2)
            + spread_matrix(shape, BLOCK, HALF // 2, HALF, 1)).astype(jnp.bfloat16)


def own_matrix():
    shape = (2 * BLOCK, COARSE)
    return (spread_matrix(shape, 0, 0, 2 * BLOCK, 1)
            + spread_matrix(shape, 0, BLOCK, 2 * BLOCK, 2)).astype(jnp.bfloat16)


def split(rows):
    high = rows.astype(jnp.bfloat16)
    return high, (rows - high.astype(jnp.float32)).astype(jnp.bfloat16)


def kernel(queries, keys, values, cotangent, att_ref, gq_ref, gk_ref, gv_ref,
           q_ref, do_ref, kv, grad, bias, mats, back_out, arrived, pass_on, ret_out,
           load_sem, sib_send, sib_recv, send_sem, recv_sem):
    count = lax.axis_size("seq")
    me = lax.axis_index("seq")
    side = lax.rem(me, 2)
    chip = me // 2
    odd = lax.rem(chip, 2)
    sib = me + 1 - 2 * side
    p_role = lax.rem(side + chip, 2)
    d_role = 1 - p_role
    is_p = p_role == 1
    is_d = p_role == 0
    peer = 2 * (chip + 1 - 2 * odd) + 1 - side
    step = 4 - 8 * odd
    has_next = (me + step >= 0) & (me + step < count)
    has_prev = (me - step >= 0) & (me - step < count)
    has_outer = is_p | has_prev
    has_far = is_d | has_prev
    d_next = is_d & has_next
    d_prev = is_d & has_prev
    p_next = is_p & has_next
    feat = queries.shape[1]
    width = feat // CHUNKS
    heads = width // HEAD_DIM
    scale = HEAD_DIM ** -0.5
    inner_start = pl.multiple_of(BLOCK * (1 - side), BLOCK)
    outer_start = pl.multiple_of(BLOCK * side, BLOCK)
    inner_half = pl.multiple_of(HALF * (1 - side), HALF)
    landing = pl.multiple_of(OUT + (RELAY - OUT) * d_role, BLOCK)
    other = pl.multiple_of(OUT + (RELAY - OUT) * p_role, BLOCK)
    top = pl.multiple_of(BACK * (1 - side), HALF)
    bottom = pl.multiple_of(BACK * side, HALF)

    loads = [pltpu.make_async_copy(src, dst, load_sem.at[i]) for i, (src, dst) in enumerate((
        (keys, kv.at[0, 0:2 * BLOCK]), (values, kv.at[1, 0:2 * BLOCK]), (queries, q_ref), (cotangent, do_ref)))]
    for item in loads:
        item.start()

    barrier = pltpu.get_barrier_semaphore()

    def greet(target):
        pl.semaphore_signal(barrier, inc=1, device_id={"seq": target}, device_id_type=MESH)

    greet(sib)
    greet(peer)

    @pl.when(d_next)
    def _():
        greet(me + step)

    @pl.when(p_next)
    def _():
        greet(sib + step)

    @pl.when(d_prev)
    def _():
        greet(me - step)
        greet(sib - step)

    def pool_own(first, number):
        cols = pl.ds(first * width, number * width)
        for which in range(2):
            half = pooled(kv[which, 0:2 * BLOCK, cols])
            kv[which, OWN_COARSE:OWN_COARSE + BLOCK, cols] = half
            kv[which, OWN_L2:OWN_L2 + HALF, cols] = pooled(half)

    loads[0].wait()
    loads[1].wait()

    peers = 2 + has_next.astype(jnp.int32) + 2 * d_prev.astype(jnp.int32)
    pl.semaphore_wait(barrier, peers)

    def remote(src, dst, sends, recvs, target):
        return pltpu.make_async_remote_copy(
            src_ref=src, dst_ref=dst, send_sem=sends, recv_sem=recvs,
            device_id={"seq": target}, device_id_type=MESH)

    def copy(stage, g, src, src_row, dst, dst_row, rows, target):
        cols = pl.ds(g * width, width)
        return remote(src.at[:, pl.ds(src_row, rows), cols], dst.at[:, pl.ds(dst_row, rows), cols],
                      send_sem.at[stage, g], recv_sem.at[stage, g], target)

    def sib_copy(kind, piece):
        cols = pl.ds(piece * (feat // PIECES), feat // PIECES)
        src, dst, rows = ((inner_start, SIB_FINE, BLOCK), (OWN_COARSE, SIB_COARSE, COARSE))[kind]
        return remote(kv.at[:, pl.ds(src, rows), cols], kv.at[:, pl.ds(dst, rows), cols],
                      sib_send.at[kind, piece], sib_recv.at[kind, piece], sib)

    def y_fine(g):
        return copy(0, g, kv, outer_start, kv, landing, BLOCK, peer)

    def y_half(g):
        return copy(1, g, kv, OWN_COARSE + inner_half, kv, landing + BLOCK, HALF, peer)

    def z_rows(g):
        return copy(2, g, kv, RELAY, kv, OUT, MESSAGE, me + step)

    def second(g):
        return copy(3, g, kv, landing + SECOND, kv, OUT + SECOND + HALF, HALF, sib + step * p_role)

    def far(g):
        return copy(4, g, kv, OUT + SECOND, kv, FAR, BLOCK, sib)

    def back(g):
        return copy(5, g, back_out, 0, arrived, 0, BACK, sib)

    def z_grads(g):
        return copy(6, g, pass_on.at[0], 0, pass_on.at[1], 0, MESSAGE, me - step)

    def second_grads(g):
        return copy(7, g, pass_on.at[0], MESSAGE, pass_on.at[1], MESSAGE, HALF, sib - step * d_role)

    def ret(g):
        return copy(8, g, ret_out, 0, arrived, BACK, MESSAGE, peer)

    sends_second = is_d | p_next
    gets_second = is_p | d_prev

    for g in range(CHUNKS):
        if g == EARLY:
            pool_own(EARLY, CHUNKS - EARLY)
        if g == 0:
            for early in range(EARLY):
                y_fine(early).start()
            pool_own(0, EARLY)
        y_half(g).start()
        if EARLY <= g + 1 < CHUNKS:
            y_fine(g + 1).start()
    for piece in range(PIECES):
        sib_copy(0, piece).start()
        sib_copy(1, piece).start()

    @pl.when(jnp.logical_not(has_outer))
    def _():
        kv[:, OUT:OUT + 3 * BLOCK, :] = jnp.zeros((2, 3 * BLOCK, feat), jnp.bfloat16)

    @pl.when(is_d & jnp.logical_not(has_next))
    def _():
        pass_on[1, :, 0:MESSAGE, :] = jnp.zeros((2, MESSAGE, feat), jnp.bfloat16)

    @pl.when(is_p & jnp.logical_not(has_next))
    def _():
        pass_on[1, :, MESSAGE:MESSAGE + HALF, :] = jnp.zeros((2, HALF, feat), jnp.bfloat16)

    lane = lax.broadcasted_iota(jnp.int32, (BLOCK, 2 * BLOCK), 1)
    is_outer_lane = (lane >> 6) == side
    zero = jnp.zeros((BLOCK, 2 * BLOCK), jnp.float32)
    for row in (0, BLOCK):
        bias[row:row + BLOCK] = zero
    bias[SIB_FINE:SIB_FINE + BLOCK] = jnp.where(is_outer_lane, masked_score, zero)
    for row in (OWN_COARSE, SIB_COARSE):
        bias[row:row + BLOCK] = zero + 1.0
        bias[row + BLOCK:row + COARSE] = zero[:HALF] + 2.0
    bias[OUT:OUT + BLOCK] = jnp.where(is_outer_lane & has_outer, zero, masked_score)
    bias[OUT + BLOCK:OUT + 2 * BLOCK] = jnp.where(has_outer, zero + 1.0, masked_score)
    bias[OUT + SECOND:OUT + 3 * BLOCK] = jnp.where(has_outer, zero + 2.0, masked_score)
    bias[FAR:FAR + BLOCK] = jnp.where(has_far, zero + 2.0, masked_score)

    message = message_matrix()
    mats[M_MESSAGE:M_MESSAGE + MESSAGE, 0:2 * BLOCK] = jnp.concatenate([message, message], axis=1)
    own = own_matrix()
    inner = spread_matrix((2 * BLOCK, HALF), inner_start, 0, BLOCK, 1).astype(jnp.bfloat16)
    mats[M_OWN:M_OWN + 2 * BLOCK, 0:2 * COARSE + HALF] = jnp.concatenate([own, inner, own], axis=1)
    mats[M_SECOND:M_SECOND + MESSAGE, 0:HALF] = second_matrix()
    mats[M_POOL:M_POOL + HALF, 0:BLOCK] = pool_matrix(BLOCK)

    def columns(g):
        return pl.ds(g * width, width)

    def derive(base, g):
        cols = columns(g)
        pool = mats[M_POOL:M_POOL + HALF, 0:BLOCK]
        for which in range(2):
            first = nn(pool, kv[which, pl.ds(base, BLOCK), cols]).astype(jnp.bfloat16)
            both = jnp.concatenate([first, kv[which, pl.ds(base + BLOCK, HALF), cols]], axis=0)
            kv[which, pl.ds(base + DERIVED, HALF), cols] = first
            kv[which, pl.ds(base + SECOND, HALF), cols] = nn(pool, both).astype(jnp.bfloat16)

    def store_parts(which, part, cols):
        for dst, src, rows in ((0, 0, 2 * BLOCK), (G_COARSE, OWN_COARSE, COARSE), (G_OUT, OUT, 3 * BLOCK)):
            grad[which, dst:dst + rows, cols] = part[src:src + rows]
        for dst, src, rows in ((0, SIB_FINE, BLOCK), (BLOCK, SIB_COARSE, COARSE), (B_FAR, FAR, BLOCK)):
            back_out[which, dst:dst + rows, cols] = part[src:src + rows].astype(jnp.bfloat16)

    def attend(first, number):
        def score(h):
            cols = pl.ds(h * HEAD_DIM, HEAD_DIM)
            scores = nt(kv[0, 0:CAND, cols], q_ref[:, cols]) * (scale * math.log2(math.e)) + bias[...]
            grad_weights = nt(kv[1, 0:CAND, cols], do_ref[:, cols])
            return scores, grad_weights, jnp.max(scores, axis=0, keepdims=True)

        def weigh(scores, grad_weights, largest):
            raised = jnp.exp2(scores - largest)
            weights = raised * (1.0 / jnp.sum(raised, axis=0, keepdims=True))
            row_dots = jnp.sum(weights * grad_weights, axis=0, keepdims=True)
            grad_scores = weights * ((grad_weights - row_dots) * scale)
            return weights.astype(jnp.bfloat16), grad_scores.astype(jnp.bfloat16)

        def combine(h, weights_b, grad_scores):
            cols = pl.ds(h * HEAD_DIM, HEAD_DIM)
            att_ref[:, cols] = tn(weights_b, kv[1, 0:CAND, cols]).astype(jnp.bfloat16)
            store_parts(1, nn(weights_b, do_ref[:, cols]), cols)
            gq_ref[:, cols] = tn(grad_scores, kv[0, 0:CAND, cols]).astype(jnp.bfloat16)
            store_parts(0, nn(grad_scores, q_ref[:, cols]), cols)

        fronts = [score(first + i) for i in range(number)]
        for i, front in enumerate(fronts):
            combine(first + i, *weigh(*front))

    def fold(g):
        cols = columns(g)
        matrix = mats[M_MESSAGE:M_MESSAGE + MESSAGE, 0:2 * BLOCK]
        for which in range(2):
            second = (grad[which, G_OUT + SECOND:GRAD_ROWS, cols]
                      + arrived[which, B_FAR:BACK, cols].astype(jnp.float32))
            coarse = jnp.concatenate([grad[which, G_OUT + DERIVED:G_OUT + SECOND, cols], second[:HALF]], axis=0)
            total = nn(matrix, jnp.concatenate(split(coarse), axis=0)) + grad[which, G_OUT:G_OUT + MESSAGE, cols]
            pass_on[0, which, 0:MESSAGE, cols] = total.astype(jnp.bfloat16)
            pass_on[0, which, MESSAGE:MESSAGE + HALF, cols] = second[HALF:].astype(jnp.bfloat16)

    def gather(g):
        cols = columns(g)
        matrix = mats[M_SECOND:M_SECOND + MESSAGE, 0:HALF]
        for which in range(2):
            total = nn(matrix, pass_on[1, which, MESSAGE:MESSAGE + HALF, cols])
            total += pass_on[d_role, which, 0:MESSAGE, cols].astype(jnp.float32)
            ret_out[which, :, cols] = total.astype(jnp.bfloat16)

    def finish(g):
        cols = columns(g)
        matrix = mats[M_OWN:M_OWN + 2 * BLOCK, 0:2 * COARSE + HALF]
        for which, ref in enumerate((gk_ref, gv_ref)):
            coarse = (grad[which, G_COARSE:G_OUT, cols]
                      + arrived[which, BLOCK:BLOCK + COARSE, cols].astype(jnp.float32))
            high, low = split(coarse)
            parts = jnp.concatenate([high, arrived[which, BACK + BLOCK:IN_ROWS, cols], low], axis=0)
            fine = jnp.concatenate([arrived[which, pl.ds(top, BLOCK), cols],
                                    arrived[which, pl.ds(bottom, BLOCK), cols]], axis=0)
            total = nn(matrix, parts) + (grad[which, 0:2 * BLOCK, cols] + fine.astype(jnp.float32))
            ref[:, cols] = total.astype(jnp.bfloat16)

    def when(cond, item, act):
        @pl.when(cond)
        def _():
            getattr(item, act)()

    loads[2].wait()
    loads[3].wait()
    for i in range(CHUNKS + LAST):
        def now(lag):
            return 0 <= i - lag < CHUNKS

        if now(0):
            y_fine(i).wait_recv()
            y_half(i).wait_recv()
            when(d_next, z_rows(i), "start")
        if now(SHARE):
            when(d_prev, z_rows(i - SHARE), "wait_recv")
            when(gets_second, second(i - SHARE), "wait_recv")
        if now(0):
            derive(landing, i)
        if now(SHARE):
            derive(other, i - SHARE)
            far(i - SHARE).start()
        if now(0):
            when(sends_second, second(i), "start")
        if now(PEER) and i - PEER < AHEAD:
            when(d_next, z_grads(i - PEER), "wait_recv")
            when(sends_second, second_grads(i - PEER), "wait_recv")
            gather(i - PEER)
            ret(i - PEER).start()
        if now(ATTEND):
            g = i - ATTEND
            if g % (CHUNKS // PIECES) == 0:
                for kind in range(2):
                    sib_copy(kind, g // (CHUNKS // PIECES)).wait_recv()
            far(g).wait_recv()
            attend(g * heads, heads)
            back(g).start()
        if now(OUTER):
            back(i - OUTER).wait_recv()
            fold(i - OUTER)
            when(d_prev, z_grads(i - OUTER), "start")
            when(gets_second, second_grads(i - OUTER), "start")
        if now(PEER) and i - PEER >= AHEAD:
            when(d_next, z_grads(i - PEER), "wait_recv")
            when(sends_second, second_grads(i - PEER), "wait_recv")
            gather(i - PEER)
            ret(i - PEER).start()
        if now(LAST):
            ret(i - LAST).wait_recv()
            finish(i - LAST)

    for piece in range(PIECES):
        for kind in range(2):
            sib_copy(kind, piece).wait_send()
    for g in range(CHUNKS):
        for item in (y_fine, y_half, far, back, ret):
            item(g).wait_send()
        when(sends_second, second(g), "wait_send")
        when(d_next, z_rows(g), "wait_send")
        when(d_prev, z_grads(g), "wait_send")
        when(gets_second, second_grads(g), "wait_send")


def place(*refs):
    sems = refs[8]
    stores = [pltpu.make_async_copy(refs[i], refs[4 + i], sems.at[i]) for i in range(4)]
    for item in stores:
        item.start()
    for item in stores:
        item.wait()


def body(queries, key_input, value_input, cotangent):
    rows, feat = queries.shape
    out = jax.ShapeDtypeStruct((rows, feat), jnp.bfloat16)
    results = pl.pallas_call(
        kernel,
        name="hier_attention",
        out_shape=[pltpu.VMEM((rows, feat), jnp.bfloat16)] * 4,
        in_specs=[pl.BlockSpec(memory_space=pl.ANY)] * 4,
        out_specs=[pl.BlockSpec(memory_space=pltpu.VMEM)] * 4,
        scratch_shapes=[
            pltpu.VMEM((rows, feat), jnp.bfloat16),
            pltpu.VMEM((rows, feat), jnp.bfloat16),
            pltpu.VMEM((2, KV_ROWS, feat), jnp.bfloat16),
            pltpu.VMEM((2, GRAD_ROWS, feat), jnp.float32),
            pltpu.VMEM((CAND, rows), jnp.float32),
            pltpu.VMEM((M_ROWS, 2 * rows), jnp.bfloat16),
            pltpu.VMEM((2, BACK, feat), jnp.bfloat16),
            pltpu.VMEM((2, IN_ROWS, feat), jnp.bfloat16),
            pltpu.VMEM((2, 2, MESSAGE + HALF, feat), jnp.bfloat16),
            pltpu.VMEM((2, MESSAGE, feat), jnp.bfloat16),
            pltpu.SemaphoreType.DMA((4,)),
            pltpu.SemaphoreType.DMA((2, PIECES)),
            pltpu.SemaphoreType.DMA((2, PIECES)),
            pltpu.SemaphoreType.DMA((STAGES, CHUNKS)),
            pltpu.SemaphoreType.DMA((STAGES, CHUNKS)),
        ],
        compiler_params=pltpu.CompilerParams(
            collective_id=0, has_side_effects=True, vmem_limit_bytes=40 * 1024 * 1024),
    )(*(pltpu.with_memory_space_constraint(x, pltpu.HBM)
        for x in (queries, key_input, value_input, cotangent)))
    return tuple(pl.pallas_call(
        place,
        name="place",
        out_shape=[out] * 4,
        in_specs=[pl.BlockSpec(memory_space=pltpu.VMEM)] * 4,
        out_specs=[pl.BlockSpec(memory_space=pl.ANY)] * 4,
        scratch_shapes=[pltpu.SemaphoreType.DMA((4,))],
    )(*(pltpu.with_memory_space_constraint(x, pltpu.VMEM) for x in results)))


def solution(mesh):
    spec = P(("groups", "seq"), None)
    return jax.shard_map(
        body, mesh=mesh, in_specs=(spec,) * 4, out_specs=(spec,) * 4, check_vma=False)
```
